32 devices in a mesh: row: 8 (over z, y), col: 4 (over x, core).
Axes of the slice: x: 2, y: 2, z: 4, core: 2. Of those that a mesh axis runs over, the one named last changes fastest.
Arguments:
- basis_values: bfloat16 [4, 4096, 4096], P(None, 'row', 'col'), may hold values from -6 to 6
- density: float32 [4096, 2560], P('row'), may hold values from -1 to 1, as said below
- screen: int32 [32, 32], P('row', 'col'), may hold values 0 or 1
- atom_of_block: int32 [32], P('col'), may hold values from 0 to 63
- atom_factor: float32 [64], replicated, may hold values from 0.5 to 2
- quad_weight: float32 [4096], P('col'), may hold values from 0.5 to 2
- core_density: float32 [4096], P('col'), may hold values from 0.3 to 1
Outputs:
- xc_matrix: float32 [4096, 1536], P(('row', 'col'))
The draws below stay inside these ranges and needn't reach their ends.
Inputs may be any that keep to these rules, and one draw needn't show every extreme that they name: The density matrix is symmetric. Column block k of a row (k from 0 to 4, 512 columns each) holds the row's entries with the basis block k - 2 places further along the closed chain of 8 blocks; all other entries are zero.
All inputs are finite; a program needn't handle non-finite values. No bound on the sum of `screen` on one device may be relied on, other than what follows from the above.
Results may differ from the reference program's by a relative error of at most 0.0014.
Values may be sent and summed in bfloat16 or wider, within the bound.
No kernel may reach another device: no remote copies, remote signals or barrier semaphores. Data moves between devices by JAX's collectives and lax.ppermute only.
A program may use at most 64 MiB of HBM per device.

```python
import math
import jax
import jax.numpy as jnp
from jax import lax

BD = 512
GD = 1024
BAND = 5
SB = 128
GB = 128
ATOMS = 64
NB = 4096
NGP = 4096
N_COL = 4


def draw_density(key, part):
    blocks = NB // BD
    reach = BAND // 2
    key_off = jax.random.fold_in(key, 11)
    key_diagonal = jax.random.fold_in(key, 12)
    random_part = jnp.clip(jax.random.normal(key_off, (blocks, BD, BAND, BD), jnp.float32), -3.0, 3.0)
    diagonal = jax.random.uniform(key_diagonal, (NB,), jnp.float32, 0.5, 1.5)
    pieces = []
    for column in range(BAND):
        mirror = jnp.roll(random_part[:, :, BAND - 1 - column, :], -(column - reach), axis=0)
        pieces.append(0.5 * (random_part[:, :, column, :] + jnp.swapaxes(mirror, 1, 2)))
    banded = jnp.stack(pieces, axis=2)
    off_scale = 0.43 / jnp.sqrt(jnp.float32(NB * BAND * BD))
    banded = off_scale * banded
    identity = jnp.eye(BD, dtype=jnp.float32)
    diagonal_part = diagonal.reshape(blocks, BD)[:, :, None] * identity[None, :, :] / NB
    banded = banded.at[:, :, reach, :].add(diagonal_part)
    return banded.reshape(NB, BAND * BD).astype(jnp.float32)


def touch_ends(result, own_key, smallest, high):
    index_at = [jax.random.randint(jax.random.fold_in(own_key, axis), (), 0, length) for axis, length in enumerate(result.shape)]
    main_axis = result.shape.index(max(result.shape))
    neighbour = index_at[:main_axis] + [(index_at[main_axis] + 1) % result.shape[main_axis]] + index_at[main_axis + 1:]
    return result.at[tuple(index_at)].set(smallest).at[tuple(neighbour)].set(high)


def block_levels(key, dims, cuts, smallest, largest):
    factor_of, own = 1.0, jax.random.fold_in(key, 6)
    for position, parts in cuts:
        steps = jnp.exp(jax.random.uniform(jax.random.fold_in(own, position), (parts,), jnp.float32, smallest / len(cuts), largest / len(cuts)))
        factor_of = factor_of * jnp.repeat(steps, dims[position] // parts).reshape([-1 if axis == position else 1 for axis in range(len(dims))])
    return factor_of


def noise(key, dims, scale, limit, shards=(), kind=jnp.bfloat16):
    result = jax.random.normal(key, dims, jnp.float32) * scale
    if len(shards) > 0:
        result = block_levels(key, dims, shards, -0.22, 0.18) * result
    return jnp.clip(result, min=-limit, max=limit).astype(kind)


def setup_inputs(seed: int = 0) -> dict:
    key_of = jax.random.split(jax.random.key(seed), 8)
    return {
        "basis_values": noise(key_of[0], (4, NB, NGP), 1.0, 6.0, ((1, 8), (2, 4))),
        "density": draw_density(jax.random.fold_in(key_of[7], 71), 0),
        "screen": touch_ends((jax.random.randint(key_of[2], (NB // SB, NGP // GB), 0, 4) < 3).astype(jnp.int32), jax.random.fold_in(key_of[2], 1), 0, 1),
        "atom_of_block": touch_ends(jax.random.randint(key_of[3], (NGP // GB,), 0, ATOMS), jax.random.fold_in(key_of[3], 1), 0, ATOMS - 1).astype(jnp.int32),
        "atom_factor": jnp.clip(jnp.exp(jax.random.uniform(key_of[4], (ATOMS,), jnp.float32, math.log(0.5), math.log(2.0))), 0.5, 2.0),
        "quad_weight": jnp.clip(jnp.exp(math.log(2.0) - 1.3862944 * jax.random.uniform(key_of[5], (NGP,), jnp.float32) ** block_levels(key_of[5], (NGP,), ((0, 4),), -0.2, 0.2)), 0.5, 2.0),
        "core_density": jnp.clip(jnp.exp(math.log(1.0) - 1.2039728 * jax.random.uniform(key_of[6], (NGP,), jnp.float32) ** block_levels(key_of[6], (NGP,), ((0, 4),), -0.2, 0.2)), 0.3, 1.0),
    }


KAPPA_VALUE = 0.804
MU_VALUE = 0.22
SLATER_COEF = 0.7386

def energy_density(density_in, squared_in, core):
    regular = jnp.sqrt(density_in * density_in + core * core)
    reduced = squared_in * regular ** (-8.0 / 3.0)
    enhance = 1.0 + KAPPA_VALUE - KAPPA_VALUE / (1.0 + MU_VALUE * reduced / KAPPA_VALUE)
    return -SLATER_COEF * regular ** (4.0 / 3.0) * enhance

def potentials(density_in, squared_in, core):

    def total_energy(first_arg, second_arg):
        return jnp.sum(energy_density(first_arg, second_arg, core))
    return jax.grad(total_energy, argnums=(0, 1))(density_in, squared_in)

def reference(basis_values, density, screen, atom_of_block, atom_factor, quad_weight, core_density):
    blocks = NB // BD
    reach = BAND // 2
    banded = density.reshape(blocks, BD, BAND, BD)
    factors = atom_factor[atom_of_block]
    per_block = GD // GB

    def grid_block(totals, index):
        first_point = index * GD
        basis = lax.dynamic_slice_in_dim(basis_values, first_point, GD, 2)
        keeper = lax.dynamic_slice_in_dim(screen, index * per_block, per_block, 1)
        masked = (basis.reshape(4, NB // SB, SB, per_block, GB) * keeper.astype(basis.dtype)[None, :, None, :, None]).reshape(4, NB, GD)
        value32 = masked[0].astype(jnp.float32).reshape(blocks, BD, GD)
        applied = jnp.zeros((blocks, BD, GD), jnp.float32)
        for column in range(BAND):
            applied = applied + jnp.einsum('rij,rjg->rig', banded[:, :, column, :], jnp.roll(value32, -(column - reach), axis=0), precision=lax.Precision.HIGHEST)
        applied = applied.reshape(NB, GD)
        masked32 = masked.astype(jnp.float32)
        sums = jnp.einsum('cmg,mg->cg', masked32, applied, precision=lax.Precision.HIGHEST)
        point_density = sums[0]
        gradient = 2.0 * sums[1:]
        squared = lax.optimization_barrier(jnp.sum(gradient * gradient, axis=0))
        block_factor = lax.dynamic_slice_in_dim(factors, index * per_block, per_block, 0)
        quad = lax.dynamic_slice_in_dim(quad_weight, first_point, GD, 0)
        weights = (quad.reshape(per_block, GB) * block_factor[:, None]).reshape(GD) / math.sqrt(NGP)
        core = lax.dynamic_slice_in_dim(core_density, first_point, GD, 0)
        density_pot, gradient_pot = potentials(point_density, squared, core)
        scalar_part = 0.5 * weights * density_pot
        vector_part = 2.0 * weights * gradient_pot * gradient
        half_pot = (scalar_part * masked32[0] + lax.optimization_barrier(jnp.sum(vector_part[:, None, :] * masked32[1:], axis=0))).astype(jnp.bfloat16)
        half32 = half_pot.astype(jnp.float32).reshape(blocks, BD, GD)
        pieces = []
        for column in range(reach + 1):
            first_term = jnp.einsum('rig,rjg->rij', half32, jnp.roll(value32, -column, axis=0), precision=lax.Precision.HIGHEST)
            second_term = jnp.einsum('rig,rjg->rij', value32, jnp.roll(half32, -column, axis=0), precision=lax.Precision.HIGHEST)
            pieces.append(first_term + second_term)
        return (totals + jnp.stack(pieces, axis=2), None)
    start_totals = jnp.zeros((blocks, BD, reach + 1, BD), jnp.float32)
    totals, ignored = lax.scan(grid_block, start_totals, jnp.arange(N_COL, dtype=jnp.int32))
    return totals.reshape(NB, (reach + 1) * BD)
```

```python
import math

import jax
import jax.numpy as jnp
from jax import lax
from jax.sharding import PartitionSpec as P

BAND = 5
CHUNKS = 4

KAPPA_VALUE = 0.804
MU_VALUE = 0.22
SLATER_COEF = 0.7386


def from_ahead(block, axis, distance):
    size = lax.axis_size(axis)
    return lax.ppermute(block, axis, [((i + distance) % size, i) for i in range(size)])


def swap(block, axis, bit):
    return lax.ppermute(block, axis, [(i, i ^ bit) for i in range(lax.axis_size(axis))])


def energy_density(density_in, squared_in, core):
    regular = jnp.sqrt(density_in * density_in + core * core)
    reduced = squared_in * regular ** (-8.0 / 3.0)
    enhance = 1.0 + KAPPA_VALUE - KAPPA_VALUE / (1.0 + MU_VALUE * reduced / KAPPA_VALUE)
    return -SLATER_COEF * regular ** (4.0 / 3.0) * enhance


def potentials(density_in, squared_in, core):

    def total_energy(first_arg, second_arg):
        return jnp.sum(energy_density(first_arg, second_arg, core))

    return jax.grad(total_energy, argnums=(0, 1))(density_in, squared_in)


def masked_basis(basis_values, screen):
    components, row_count, points = basis_values.shape
    row_blocks, point_blocks = screen.shape
    shaped = basis_values.reshape(
        components, row_blocks, row_count // row_blocks, point_blocks, points // point_blocks
    )
    keeper = screen.astype(basis_values.dtype)[None, :, None, :, None]
    return (shaped * keeper).reshape(components, row_count, points)


def contract(left_side, right_side):
    return lax.dot_general(
        left_side, right_side, (((1,), (1,)), ((), ())), preferred_element_type=jnp.float32
    )


def body(basis_values, density, screen, atom_of_block, atom_factor, quad_weight, core_density):
    rows, cols = lax.axis_size("row"), lax.axis_size("col")
    odd = lax.axis_index("row") % 2 == 1
    col = lax.axis_index("col")
    masked = masked_basis(basis_values, screen)
    values = masked[0]
    row_count, points = values.shape
    reach = BAND // 2
    width = points // CHUNKS

    def strip(offset):
        return density[:, (offset + reach) * row_count : (offset + reach + 1) * row_count]

    strip_beside = jnp.where(odd, strip(-1), strip(1))
    strip_across = jnp.where(odd, strip(1), strip(-1))
    masked32 = masked.astype(jnp.float32)
    gathered = {name: [] for name in ("ahead", "behind", "beside", "across")}
    sums = []
    for chunk in range(CHUNKS):
        window = slice(chunk * width, (chunk + 1) * width)
        own = values[:, window]
        ahead = from_ahead(own, "row", 2)
        behind = from_ahead(own, "row", -2)
        beside = swap(own, "row", 1)
        across = swap(jnp.where(odd, behind, ahead), "row", 1)
        applied = jnp.zeros((row_count, width), jnp.float32)
        for piece, block in (
            (strip(0), own),
            (strip_beside, beside),
            (strip(2), ahead),
            (strip(-2), behind),
            (strip_across, across),
        ):
            applied = applied + jnp.dot(
                piece, block.astype(jnp.float32), precision=lax.Precision.HIGHEST
            )
        sums.append(
            jnp.einsum(
                "cmg,mg->cg", masked32[:, :, window], applied, precision=lax.Precision.HIGHEST
            )
        )
        for name, block in (
            ("ahead", ahead), ("behind", behind), ("beside", beside), ("across", across)
        ):
            gathered[name].append(block)
    summed = jnp.concatenate(sums, axis=1)
    bit = 1
    while bit < rows:
        summed = summed + swap(summed, "row", bit)
        bit *= 2
    blocks = {name: jnp.concatenate(parts, axis=1) for name, parts in gathered.items()}
    nearby = {
        1: jnp.where(odd, blocks["across"], blocks["beside"]),
        -1: jnp.where(odd, blocks["beside"], blocks["across"]),
        2: blocks["ahead"],
        -2: blocks["behind"],
    }

    point_density = summed[0]
    gradient = 2.0 * summed[1:]
    squared = jnp.sum(gradient * gradient, axis=0)
    atoms = atom_factor.shape[0]
    chooser = (atom_of_block[:, None] == jnp.arange(atoms, dtype=jnp.int32)[None, :]).astype(
        jnp.float32
    )
    block_factor = jnp.dot(chooser, atom_factor, precision=lax.Precision.HIGHEST)
    group_size = points // atom_of_block.shape[0]
    weights = (quad_weight.reshape(-1, group_size) * block_factor[:, None]).reshape(
        points
    ) / math.sqrt(points * cols)
    density_pot, gradient_pot = potentials(point_density, squared, core_density)
    scalar_part = 0.5 * weights * density_pot
    vector_part = 2.0 * weights * gradient_pot * gradient
    half_pot = (
        scalar_part * masked32[0] + jnp.sum(vector_part[:, None, :] * masked32[1:], axis=0)
    ).astype(jnp.bfloat16)

    share = row_count // cols

    def scatter(product, link_type):
        pieces = product.reshape(cols, share, product.shape[1])
        bit = 1
        while bit < cols:
            paired = pieces.reshape(-1, 2, *pieces.shape[1:])
            mine = (col // bit) % 2
            keep = lax.dynamic_index_in_dim(paired, mine, 1, keepdims=False)
            send = lax.dynamic_index_in_dim(paired, 1 - mine, 1, keepdims=False)
            if bit > 1:
                send = send.astype(link_type)
            pieces = keep + swap(send, "col", bit).astype(jnp.float32)
            bit *= 2
        return pieces[0]

    mirrored = [contract(nearby[-offset], half_pot) for offset in range(1, reach + 1)]
    direct = [contract(half_pot, nearby[offset]) for offset in range(1, reach + 1)]
    central = contract(half_pot, values) + contract(values, half_pot)
    mirrored = [scatter(block, jnp.bfloat16) for block in mirrored]
    mirrored = [
        from_ahead(block.astype(jnp.bfloat16), "row", offset + 1).astype(jnp.float32)
        for offset, block in enumerate(mirrored)
    ]
    direct = [scatter(block, jnp.bfloat16) for block in direct]
    central = scatter(central, jnp.float32)
    return jnp.concatenate([central] + [d + m for d, m in zip(direct, mirrored)], axis=1)


def solution(mesh):
    in_specs = (
        P(None, "row", "col"),
        P("row", None),
        P("row", "col"),
        P("col"),
        P(),
        P("col"),
        P("col"),
    )
    out_specs = P(("row", "col"), None)
    return jax.shard_map(body, mesh=mesh, in_specs=in_specs, out_specs=out_specs, check_vma=False)
```

```python
import functools
import math

import jax
import jax.numpy as jnp
from jax import lax
from jax.experimental import pallas as pl
from jax.experimental.pallas import tpu as pltpu
from jax.sharding import PartitionSpec as P

BAND = 5
REACH = BAND // 2
CHUNKS = 4

KAPPA_VALUE = 0.804
MU_VALUE = 0.22
SLATER_COEF = 0.7386


WHOLE = pl.BlockSpec(memory_space=pltpu.VMEM)
SCALARS = pl.BlockSpec(memory_space=pltpu.SMEM)
F32 = jnp.float32
BF16 = jnp.bfloat16


def from_ahead(block, distance):
    size = lax.axis_size("row")
    return lax.ppermute(block, "row", [((i + distance) % size, i) for i in range(size)])


def from_side(block, distance):
    size = lax.axis_size("row")
    route = [((i + (distance if i % 2 == 0 else -distance)) % size, i) for i in range(size)]
    return lax.ppermute(block, "row", route)


def swap(block, axis, bit):
    return lax.ppermute(block, axis, [(i, i ^ bit) for i in range(lax.axis_size(axis))])


def energy_density(density_in, squared_in, core):
    regular = jnp.sqrt(density_in * density_in + core * core)
    reduced = squared_in * regular ** (-8.0 / 3.0)
    enhance = 1.0 + KAPPA_VALUE - KAPPA_VALUE / (1.0 + MU_VALUE * reduced / KAPPA_VALUE)
    return -SLATER_COEF * regular ** (4.0 / 3.0) * enhance


def potentials(density_in, squared_in, core):

    def total_energy(first_arg, second_arg):
        return jnp.sum(energy_density(first_arg, second_arg, core))

    return jax.grad(total_energy, argnums=(0, 1))(density_in, squared_in)


def call(kernel, outs, in_specs, flops, bytes_accessed, out_specs=None, scratch=()):
    return pl.pallas_call(
        kernel,
        out_shape=outs,
        in_specs=in_specs,
        out_specs=jax.tree.map(lambda _: WHOLE, outs) if out_specs is None else out_specs,
        scratch_shapes=list(scratch),
        cost_estimate=pl.CostEstimate(
            flops=int(flops), bytes_accessed=int(bytes_accessed), transcendentals=0
        ),
    )


def dot(left, right):
    return jnp.dot(left, right, preferred_element_type=F32)


def dot_rows(left, right):
    return lax.dot_general(left, right, (((1,), (1,)), ((), ())), preferred_element_type=F32)


def mask_kernel(sb, gb, width, screen_ref, basis_ref, *chunk_refs):
    row_blocks = basis_ref.shape[1] // sb
    for index, out in enumerate(chunk_refs):
        for part in range(width // gb):
            col = index * width + part * gb
            for row in range(row_blocks):
                keep = screen_ref[row, col // gb].astype(F32)
                tile = basis_ref[0, row * sb : (row + 1) * sb, col : col + gb].astype(F32)
                out[row * sb : (row + 1) * sb, part * gb : (part + 1) * gb] = (tile * keep).astype(
                    BF16
                )


def split_kernel(density_ref, high_ref, low_ref):
    size = density_ref.shape[0]
    for column in range(BAND):
        strip = density_ref[:, column * size : (column + 1) * size]
        high = strip.astype(BF16)
        high_ref[column] = high
        low_ref[column] = (strip - high.astype(F32)).astype(BF16)


def applied_kernel(place_ref, high_ref, low_ref, own, beside, near, far, total_ref):
    sign = 1 - 2 * place_ref[0]
    total = dot(high_ref[REACH], own[...]) + dot(low_ref[REACH], own[...])
    for block, offset in ((beside, 1), (near, 2), (far, -2)):
        column = REACH + sign * offset
        total += dot(high_ref[column], block[...]) + dot(low_ref[column], block[...])
    total_ref[...] = total


def sums_kernel(
    sb, gb, first, place_ref, screen_ref, high_ref, low_ref, across, partial_ref, basis_ref, sums_ref,
    total_ref,
):
    column = REACH - (1 - 2 * place_ref[0])
    total_ref[...] = (
        partial_ref[...] + dot(high_ref[column], across[...]) + dot(low_ref[column], across[...])
    )
    components, row_count, width = basis_ref.shape
    for part in range(width // gb):
        cols = slice(part * gb, (part + 1) * gb)
        found = [jnp.zeros((1, gb), F32) for _ in range(components)]
        for row in range(row_count // sb):
            rows = slice(row * sb, (row + 1) * sb)
            keep = screen_ref[row, first + part].astype(F32)
            applied = total_ref[rows, cols]
            for c in range(components):
                product = basis_ref[c, rows, cols].astype(F32) * applied
                found[c] += keep * jnp.sum(product, axis=0, keepdims=True)
        for c in range(components):
            sums_ref[c : c + 1, cols] = found[c]


def sort_kernel(place_ref, beside, near, across, far, forward_ref, backward_ref):
    for index, (first, second) in enumerate(((beside, across), (near, far))):

        @pl.when(place_ref[0] == 0)
        def _():
            forward_ref[index] = first[...]
            backward_ref[index] = second[...]

        @pl.when(place_ref[0] != 0)
        def _():
            forward_ref[index] = second[...]
            backward_ref[index] = first[...]


def half_kernel(sb, gb, screen_ref, basis_ref, parts_ref, half_ref):
    components, row_count, points = basis_ref.shape
    for part in range(points // gb):
        cols = slice(part * gb, (part + 1) * gb)
        for row in range(row_count // sb):
            rows = slice(row * sb, (row + 1) * sb)
            keep = screen_ref[row, part].astype(F32)
            total = (parts_ref[0:1, cols] * keep) * basis_ref[0, rows, cols].astype(F32)
            for c in range(1, components):
                total += (parts_ref[c : c + 1, cols] * keep) * basis_ref[c, rows, cols].astype(F32)
            half_ref[rows, cols] = total.astype(BF16)


def column_chunks(ref, width):
    return [ref[:, c * width : (c + 1) * width] for c in range(ref.shape[1] // width)]


def rows_of(ref, lead, first, share, count, stride):
    blocks = []
    for step in range(count):
        window = pl.ds(pl.multiple_of((first + step * stride) * share, share), share)
        blocks.append(ref[window, :] if lead is None else ref[lead, window, :])
    return jnp.concatenate(blocks, axis=0) if count > 1 else blocks[0]


def mirrored_product(half_ref, backward, width, side, share, count):
    total = 0
    for index, block in enumerate(backward):
        left = jnp.concatenate(
            [rows_of(block, k, side, share, count, 2) for k in range(REACH)], axis=0
        )
        total += dot_rows(left, half_ref[:, index * width : (index + 1) * width])
    return total.reshape(REACH, count, share, half_ref.shape[0])


def central_product(half_ref, own, width, side, share, count):
    total = 0
    for index, block in enumerate(own):
        cols = slice(index * width, (index + 1) * width)
        total += dot_rows(rows_of(block, None, side, share, count, 2), half_ref[:, cols])
        total += dot_rows(rows_of(half_ref.at[:, cols], None, side, share, count, 2), block[...])
    return total.reshape(count, share, half_ref.shape[0])


def direct_product(half_ref, forward, k, width, side, share, count):
    total = 0
    for index, block in enumerate(forward):
        cols = slice(index * width, (index + 1) * width)
        total += dot_rows(rows_of(half_ref.at[:, cols], None, side, share, count, 2), block[k])
    return total.reshape(count, share, half_ref.shape[0])


def mirrored_other_kernel(width, share, count, place_ref, half_ref, *refs):
    backward, out = refs[:-1], refs[-1]
    out[...] = mirrored_product(half_ref, backward, width, 1 - place_ref[1], share, count)


def mirrored_own_kernel(width, share, count, place_ref, half_ref, found_ref, *refs):
    backward, (keep_ref, send_ref) = refs[:-2], refs[-2:]
    total = mirrored_product(half_ref, backward, width, place_ref[1], share, count)
    total_ref = found_ref
    del total_ref
    deposit(total + found_ref[...], place_ref[2], keep_ref, send_ref)


def deposit(total, side, keep_ref, send_ref):
    count = total.shape[-3]
    for step in range(count // 2):
        low, high = total[..., 2 * step, :, :], total[..., 2 * step + 1, :, :]
        keep_ref[..., step, :, :] = jnp.where(side == 0, low, high)
        send_ref[..., step, :, :] = jnp.where(side == 0, high, low).astype(send_ref.dtype)


def direct_other_kernel(width, share, count, chunks, place_ref, half_ref, *refs):
    own, forward, out = refs[:chunks], refs[chunks : 2 * chunks], refs[-1]
    side = 1 - place_ref[1]
    out[0] = central_product(half_ref, own, width, side, share, count)
    for k in range(REACH):
        out[k + 1] = direct_product(half_ref, forward, k, width, side, share, count)


def direct_own_kernel(width, share, count, chunks, place_ref, half_ref, found_ref, *refs):
    own, forward = refs[:chunks], refs[chunks : 2 * chunks]
    keep_ref, central_ref, send_ref = refs[-3:]
    side = place_ref[1]
    total = central_product(half_ref, own, width, side, share, count) + found_ref[0]
    deposit(total, place_ref[2], keep_ref.at[0], central_ref)
    for k in range(REACH):
        total = direct_product(half_ref, forward, k, width, side, share, count) + found_ref[k + 1]
        deposit(total, place_ref[2], keep_ref.at[k + 1], send_ref.at[k])


def shape(dims, kind=F32):
    return jax.ShapeDtypeStruct(dims, kind)


def body(basis_values, density, screen, atom_of_block, atom_factor, quad_weight, core_density):
    rows, cols = lax.axis_size("row"), lax.axis_size("col")
    col = lax.axis_index("col")
    place = jnp.stack(
        [lax.axis_index("row") % 2, col % 2, (col // 2) % 2]
    ).astype(jnp.int32)
    components, row_count, points = basis_values.shape
    sb, gb = row_count // screen.shape[0], points // screen.shape[1]
    width = points // CHUNKS
    share, count = row_count // cols, cols // 2

    own = pl.pallas_call(
        functools.partial(mask_kernel, sb, gb, width),
        grid=(1,),
        out_shape=[shape((row_count, width), BF16)] * CHUNKS,
        in_specs=[SCALARS, pl.BlockSpec((1, row_count, points), lambda i: (0, 0, 0))],
        out_specs=[pl.BlockSpec((row_count, width), lambda i: (0, 0))] * CHUNKS,
        cost_estimate=pl.CostEstimate(
            flops=row_count * points, bytes_accessed=4 * row_count * points, transcendentals=0
        ),
    )(screen, basis_values)
    high, low = call(
        split_kernel, [shape((BAND, row_count, row_count), BF16)] * 2, [WHOLE],
        density.size * 4, density.size * 8,
    )(density)

    sums, forward, backward = [], [], []
    for chunk in range(CHUNKS):
        mine = own[chunk]
        near = from_side(mine, 2)
        far = from_side(mine, -2)
        beside = swap(mine, "row", 1)
        across = swap(near, "row", 1)
        partial = call(
            applied_kernel, shape((row_count, width)), [SCALARS] + [WHOLE] * 6,
            16 * row_count * row_count * width, 8 * row_count * row_count * 2,
        )(place, high, low, mine, beside, near, far)
        sums.append(
            pl.pallas_call(
                functools.partial(sums_kernel, sb, gb, chunk * (width // gb)),
                grid=(1,),
                out_shape=shape((components, width)),
                in_specs=[SCALARS, SCALARS] + [WHOLE] * 4
                + [pl.BlockSpec((components, row_count, width), lambda i, c=chunk: (0, 0, c))],
                out_specs=pl.BlockSpec((components, width), lambda i: (0, 0)),
                scratch_shapes=[pltpu.VMEM((row_count, width), F32)],
                cost_estimate=pl.CostEstimate(
                    flops=4 * row_count * row_count * width,
                    bytes_accessed=4 * row_count * row_count, transcendentals=0,
                ),
            )(place, screen, high, low, across, partial, basis_values)
        )
        ahead, behind = call(
            sort_kernel, [shape((REACH, row_count, width), BF16)] * 2, [SCALARS] + [WHOLE] * 4,
            row_count * width, 16 * row_count * width,
        )(place, beside, near, across, far)
        forward.append(ahead)
        backward.append(behind)
    summed = jnp.concatenate(sums, axis=1)
    bit = 1
    while bit < rows:
        summed = summed + swap(summed, "row", bit)
        bit *= 2

    point_density = summed[0]
    gradient = 2.0 * summed[1:]
    squared = jnp.sum(gradient * gradient, axis=0)
    atoms = atom_factor.shape[0]
    chooser = (atom_of_block[:, None] == jnp.arange(atoms, dtype=jnp.int32)[None, :]).astype(F32)
    block_factor = jnp.dot(chooser, atom_factor, precision=lax.Precision.HIGHEST)
    group_size = points // atom_of_block.shape[0]
    weights = (quad_weight.reshape(-1, group_size) * block_factor[:, None]).reshape(
        points
    ) / math.sqrt(points * cols)
    density_pot, gradient_pot = potentials(point_density, squared, core_density)
    scalar_part = 0.5 * weights * density_pot
    vector_part = 2.0 * weights * gradient_pot * gradient
    parts = jnp.concatenate([scalar_part[None], vector_part], axis=0)
    half = call(
        functools.partial(half_kernel, sb, gb), shape((row_count, points), BF16),
        [SCALARS, WHOLE, WHOLE], 8 * basis_values.size, 2 * basis_values.size,
    )(screen, basis_values, parts)

    product = 2 * row_count * points * share * count
    mirrored_other = call(
        functools.partial(mirrored_other_kernel, width, share, count),
        shape((REACH, count, share, row_count)), [SCALARS] + [WHOLE] * (1 + CHUNKS),
        product * 2, 4 * row_count * points,
    )(place, half, *backward)
    mirrored_found = swap(mirrored_other, "col", 1)
    direct_other = call(
        functools.partial(direct_other_kernel, width, share, count, CHUNKS),
        shape((REACH + 1, count, share, row_count)), [SCALARS] + [WHOLE] * (1 + 2 * CHUNKS),
        product * 4, 6 * row_count * points,
    )(place, half, *own, *forward)
    direct_found = swap(direct_other, "col", 1)
    kept = count // 2
    mirrored_keep, mirrored_send = call(
        functools.partial(mirrored_own_kernel, width, share, count),
        [
            shape((REACH, kept, share, row_count)),
            shape((REACH, kept, share, row_count), BF16),
        ],
        [SCALARS] + [WHOLE] * (2 + CHUNKS), product * 2, 6 * row_count * points,
    )(place, half, mirrored_found, *backward)
    direct_keep, central_send, direct_send = call(
        functools.partial(direct_own_kernel, width, share, count, CHUNKS),
        [
            shape((REACH + 1, kept, share, row_count)),
            shape((kept, share, row_count)),
            shape((REACH, kept, share, row_count), BF16),
        ],
        [SCALARS] + [WHOLE] * (2 + 2 * CHUNKS), product * 4, 8 * row_count * points,
    )(place, half, direct_found, *own, *forward)

    def scatter(keep, send):
        axis = keep.ndim - 3
        total = keep + swap(send, "col", 2).astype(F32)
        bit = 4
        while bit < cols:
            paired = total.reshape(*total.shape[:axis], -1, 2, *total.shape[axis + 1 :])
            mine = (col // bit) % 2
            keep = lax.dynamic_index_in_dim(paired, mine, axis + 1, keepdims=False)
            send = lax.dynamic_index_in_dim(paired, 1 - mine, axis + 1, keepdims=False)
            total = keep + swap(send, "col", bit)
            bit *= 2
        return jnp.squeeze(total, axis)

    mirrored = scatter(mirrored_keep, mirrored_send).astype(BF16)
    mirrored = [from_ahead(mirrored[k], k + 1).astype(F32) for k in range(REACH)]
    central = scatter(direct_keep[0], central_send)
    direct = scatter(direct_keep[1:], direct_send)
    return jnp.concatenate([central] + [direct[k] + mirrored[k] for k in range(REACH)], axis=1)


def solution(mesh):
    in_specs = (
        P(None, "row", "col"),
        P("row", None),
        P("row", "col"),
        P("col"),
        P(),
        P("col"),
        P("col"),
    )
    out_specs = P(("row", "col"), None)
    return jax.shard_map(body, mesh=mesh, in_specs=in_specs, out_specs=out_specs, check_vma=False)
```

```python
import functools
import math

import jax
import jax.numpy as jnp
from jax import lax
from jax.experimental import pallas as pl
from jax.experimental.pallas import tpu as pltpu
from jax.sharding import PartitionSpec as P


BAND = 5
REACH = BAND // 2

KAPPA_VALUE = 0.804
MU_VALUE = 0.22
SLATER_COEF = 0.7386


WHOLE = pl.BlockSpec(memory_space=pltpu.VMEM)
SCALARS = pl.BlockSpec(memory_space=pltpu.SMEM)
ANYWHERE = pl.BlockSpec(memory_space=pl.ANY)
PARAMS = pltpu.CompilerParams(vmem_limit_bytes=20 << 20)
F32 = jnp.float32
BF16 = jnp.bfloat16


def from_ahead(block, distance):
    size = lax.axis_size("row")
    return lax.ppermute(block, "row", [((i + distance) % size, i) for i in range(size)])


def from_side(block, distance):
    size = lax.axis_size("row")
    route = [((i + (distance if i % 2 == 0 else -distance)) % size, i) for i in range(size)]
    return lax.ppermute(block, "row", route)


def swap(block, axis, bit):
    return lax.ppermute(block, axis, [(i, i ^ bit) for i in range(lax.axis_size(axis))])


def energy_density(density_in, squared_in, core):
    regular = jnp.sqrt(density_in * density_in + core * core)
    reduced = squared_in * regular ** (-8.0 / 3.0)
    enhance = 1.0 + KAPPA_VALUE - KAPPA_VALUE / (1.0 + MU_VALUE * reduced / KAPPA_VALUE)
    return -SLATER_COEF * regular ** (4.0 / 3.0) * enhance


def potentials(density_in, squared_in, core):

    def total_energy(first_arg, second_arg):
        return jnp.sum(energy_density(first_arg, second_arg, core))

    return jax.grad(total_energy, argnums=(0, 1))(density_in, squared_in)


def call(kernel, outs, in_specs, flops, bytes_accessed, out_specs=None, scratch=()):
    return pl.pallas_call(
        kernel,
        out_shape=outs,
        in_specs=in_specs,
        out_specs=jax.tree.map(lambda _: WHOLE, outs) if out_specs is None else out_specs,
        scratch_shapes=list(scratch),
        compiler_params=PARAMS,
        cost_estimate=pl.CostEstimate(
            flops=int(flops), bytes_accessed=int(bytes_accessed), transcendentals=0
        ),
    )


def dot(left, right):
    return jnp.dot(left, right, preferred_element_type=F32)


def dot_rows(left, right):
    return lax.dot_general(left, right, (((1,), (1,)), ((), ())), preferred_element_type=F32)


def position():
    col = lax.axis_index("col")
    return lax.axis_index("row") % 2, col % 2, (col // 2) % 2


def mask_kernel(sb, gb, screen_ref, basis_ref, own_ref, *rest):
    chunk_refs, (tile_ref, sems) = rest[:-2], rest[-2:]
    row_count, _ = own_ref.shape
    copies = []
    for row in range(row_count // sb):
        window = pl.ds(row * sb, sb)
        copy = pltpu.make_async_copy(basis_ref.at[0, window], tile_ref.at[window], sems.at[row])
        copy.start()
        copies.append(copy)
    for row, copy in enumerate(copies):
        rows = slice(row * sb, (row + 1) * sb)
        copy.wait()
        col = 0
        for chunk in chunk_refs:
            for start in range(0, chunk.shape[1], gb):
                keep = screen_ref[row, col // gb].astype(F32)
                tile = (tile_ref[rows, col : col + gb].astype(F32) * keep).astype(BF16)
                own_ref[rows, col : col + gb] = tile
                chunk[rows, start : start + gb] = tile
                col += gb


def split_kernel(density_ref, high_ref, low_ref):
    size = density_ref.shape[0]
    for column in range(BAND):
        strip = density_ref[:, column * size : (column + 1) * size]
        high = strip.astype(BF16)
        high_ref[column] = high
        low_ref[column] = (strip - high.astype(F32)).astype(BF16)


def both(high_ref, low_ref, column, block):
    return dot(high_ref[column], block) + dot(low_ref[column], block)


def early_kernel(high_ref, low_ref, own, beside, *rest):
    near, totals = rest[: len(rest) // 2], rest[len(rest) // 2 :]
    sign = 1 - 2 * position()[0]
    start = 0
    for block, total in zip(near, totals):
        cols = slice(start, start + block.shape[1])
        total[...] = (
            both(high_ref, low_ref, REACH, own[:, cols])
            + both(high_ref, low_ref, REACH + sign, beside[:, cols])
            + both(high_ref, low_ref, REACH + 2 * sign, block[...])
        )
        start += block.shape[1]


def sums_kernel(sb, gb, first, screen_ref, high_ref, low_ref, partial_ref, far, across, basis_ref,
                sums_ref, total_ref):
    sign = 1 - 2 * position()[0]
    total_ref[...] = (
        partial_ref[...]
        + both(high_ref, low_ref, REACH - 2 * sign, far[...])
        + both(high_ref, low_ref, REACH - sign, across[...])
    )
    components, row_count, width = basis_ref.shape[0], far.shape[0], far.shape[1]
    for part in range(width // gb):
        cols = slice(part * gb, (part + 1) * gb)
        source = slice((first + part) * gb, (first + part + 1) * gb)
        found = [jnp.zeros((1, gb), F32) for _ in range(components)]
        for row in range(row_count // sb):
            rows = slice(row * sb, (row + 1) * sb)
            keep = screen_ref[row, first + part].astype(F32)
            applied = total_ref[rows, cols]
            for c in range(components):
                product = basis_ref[c, rows, source].astype(F32) * applied
                found[c] += keep * jnp.sum(product, axis=0, keepdims=True)
        for c in range(components):
            sums_ref[c : c + 1, cols] = found[c]


def half_kernel(sb, gb, screen_ref, basis_ref, parts_ref, half_ref):
    components, row_count, points = basis_ref.shape
    for part in range(points // gb):
        cols = slice(part * gb, (part + 1) * gb)
        for row in range(row_count // sb):
            rows = slice(row * sb, (row + 1) * sb)
            keep = screen_ref[row, part].astype(F32)
            total = (parts_ref[0:1, cols] * keep) * basis_ref[0, rows, cols].astype(F32)
            for c in range(1, components):
                total += (parts_ref[c : c + 1, cols] * keep) * basis_ref[c, rows, cols].astype(F32)
            half_ref[rows, cols] = total.astype(BF16)


def rows_of(ref, cols, side, share, count):
    blocks = []
    for step in range(count):
        window = pl.ds(pl.multiple_of((2 * step + side) * share, share), share)
        blocks.append(ref[window, cols])
    return jnp.concatenate(blocks, axis=0) if count > 1 else blocks[0]


def pieces(blocks):
    start = 0
    for block in blocks:
        width = block.shape[1]
        yield slice(start, start + width), block
        start += width


def mirrored_product(half_ref, one, two, side, share, count):
    total = 0
    for blocks in zip(pieces(two), pieces(one) if len(one) > 1 else pieces(two)):
        (cols, second), (_, first) = blocks
        if len(one) > 1:
            first_rows = rows_of(first, slice(None), side, share, count)
        else:
            first_rows = rows_of(one[0], cols, side, share, count)
        left = jnp.concatenate(
            [first_rows, rows_of(second, slice(None), side, share, count)], axis=0
        )
        total += dot_rows(left, half_ref[:, cols])
    return total.reshape(REACH, count, share, half_ref.shape[0])


def central_product(half_ref, own, side, share, count):
    cols = slice(None)
    total = dot_rows(rows_of(own, cols, side, share, count), half_ref[...])
    total += dot_rows(rows_of(half_ref, cols, side, share, count), own[...])
    return total.reshape(count, share, half_ref.shape[0])


def direct_product(half_ref, blocks, side, share, count):
    total = 0
    for cols, block in pieces(blocks):
        total += dot_rows(rows_of(half_ref, cols, side, share, count), block[...])
    return total.reshape(count, share, half_ref.shape[0])


def neighbours(refs, chunks):
    beside, near = refs[:1], refs[1 : 1 + chunks]
    far, across = refs[1 + chunks : 1 + 2 * chunks], refs[1 + 2 * chunks : 1 + 3 * chunks]
    return (beside, near), (across, far)


def on_side(refs, chunks, ahead, run):
    first, second = neighbours(refs, chunks)
    odd = position()[0]

    @pl.when(odd == (0 if ahead else 1))
    def _():
        run(*first)

    @pl.when(odd == (1 if ahead else 0))
    def _():
        run(*second)


def deposit(total, side, keep_ref, send_ref):
    for step in range(total.shape[-3] // 2):
        low, high = total[..., 2 * step, :, :], total[..., 2 * step + 1, :, :]
        keep_ref[..., step, :, :] = jnp.where(side == 0, low, high)
        send_ref[..., step, :, :] = jnp.where(side == 0, high, low).astype(send_ref.dtype)


def mirrored_other_kernel(share, count, chunks, half_ref, *refs):
    refs, out = refs[:-1], refs[-1]
    side = 1 - position()[1]

    def run(one, two):
        out[...] = mirrored_product(half_ref, one, two, side, share, count)

    on_side(refs, chunks, False, run)


def mirrored_own_kernel(share, count, chunks, half_ref, found_ref, *refs):
    refs, keep_ref, send_ref = refs[:-2], refs[-2], refs[-1]
    _, core, side = position()

    def run(one, two):
        total = mirrored_product(half_ref, one, two, core, share, count)
        deposit(total + found_ref[...], side, keep_ref, send_ref)

    on_side(refs, chunks, False, run)


def direct_other_kernel(share, count, chunks, half_ref, own, earlier_ref, *refs):
    refs, out = refs[:-1], refs[-1]
    side = 1 - position()[1]
    out[0] = central_product(half_ref, own, side, share, count)

    def run(one, two):
        out[1] = direct_product(half_ref, one, side, share, count)
        out[2] = direct_product(half_ref, two, side, share, count)

    on_side(refs, chunks, True, run)


def direct_own_kernel(share, count, chunks, half_ref, own, earlier_ref, found_ref, *refs):
    refs, keep_ref, send_ref = refs[:-2], refs[-2], refs[-1]
    _, core, side = position()
    size = half_ref.shape[0]
    spare = send_ref.shape[-1] - 3 * size

    def place(k, total):
        for step in range(count // 2):
            low, high = total[2 * step], total[2 * step + 1]
            keep_ref[k, step] = jnp.where(side == 0, low, high)
            send = jnp.where(side == 0, high, low)
            rounded = send.astype(BF16)
            send_ref[step, :, k * size : (k + 1) * size] = rounded
            if k == 0:
                for block in range(size // spare):
                    quarter = (2 * step + 1 - side) * 2 + core

                    @pl.when((quarter * share) // spare == block)
                    def _():
                        cols = slice(block * spare, (block + 1) * spare)
                        rest = send[:, cols] - rounded[:, cols].astype(F32)
                        send_ref[step, :, 3 * size :] = rest.astype(BF16)

    place(0, central_product(half_ref, own, core, share, count) + found_ref[0])

    def run(one, two):
        place(1, direct_product(half_ref, one, core, share, count) + found_ref[1])
        place(2, direct_product(half_ref, two, core, share, count) + found_ref[2])

    on_side(refs, chunks, True, run)


def joined_kernel(share, keep_ref, found_ref, out_ref):
    _, core, side = position()
    size = keep_ref.shape[-1]
    spare = found_ref.shape[-1] - 3 * size
    for step in range(found_ref.shape[0]):
        for k in range(3):
            part = found_ref[step, :, k * size : (k + 1) * size].astype(F32)
            out_ref[step, :, k * size : (k + 1) * size] = keep_ref[k, step] + part
        quarter = (2 * step + side) * 2 + core
        for block in range(size // spare):

            @pl.when((quarter * share) // spare == block)
            def _():
                cols = slice(block * spare, (block + 1) * spare)
                out_ref[step, :, cols] += found_ref[step, :, 3 * size :].astype(F32)


def final_kernel(share, keep_ref, found_ref, *refs):
    mirrored, out_ref = refs[:-1], refs[-1]
    joined_kernel(share, keep_ref, found_ref, out_ref)
    size = keep_ref.shape[-1]
    for k, block in enumerate(mirrored):
        cols = slice((k + 1) * size, (k + 2) * size)
        out_ref[0, :, cols] += block[...].astype(F32)


def shape(dims, kind=F32):
    return jax.ShapeDtypeStruct(dims, kind)


def body(basis_values, density, screen, atom_of_block, atom_factor, quad_weight, core_density):
    rows, cols = lax.axis_size("row"), lax.axis_size("col")
    col = lax.axis_index("col")
    components, row_count, points = basis_values.shape
    sb, gb = row_count // screen.shape[0], points // screen.shape[1]
    last = max(1, screen.shape[1] // 4) * gb
    widths = (points - last, last)
    chunks = len(widths)
    share, count = row_count // cols, cols // 2
    square = 2 * row_count * row_count

    own, *mine = call(
        functools.partial(mask_kernel, sb, gb),
        [shape((row_count, width), BF16) for width in (points, *widths)],
        [SCALARS, pl.BlockSpec(memory_space=pltpu.HBM)], row_count * points, 6 * row_count * points,
        scratch=[
            pltpu.VMEM((row_count, points), BF16),
            pltpu.SemaphoreType.DMA((screen.shape[0],)),
        ],
    )(screen, basis_values)
    near, far, across = [], [], []
    for chunk, block in enumerate(mine):
        near.append(from_side(block, 2))
        far.append(from_side(block, -2))
        across.append(swap(near[chunk], "row", 1))
    beside = swap(own, "row", 1)

    high, low = call(
        split_kernel, [shape((BAND, row_count, row_count), BF16)] * 2, [WHOLE],
        density.size * 4, density.size * 8,
    )(density)
    partial = call(
        early_kernel, [shape((row_count, width)) for width in widths], [WHOLE] * (4 + chunks),
        6 * square * points, 10 * square,
    )(high, low, own, beside, *near)
    sums, first = [], 0
    for chunk, width in enumerate(widths):
        sums.append(
            call(
                functools.partial(sums_kernel, sb, gb, first), shape((components, width)),
                [SCALARS] + [WHOLE] * 6, 4 * square * width, 6 * square,
                scratch=[pltpu.VMEM((row_count, width), F32)],
            )(screen, high, low, partial[chunk], far[chunk], across[chunk], basis_values)
        )
        first += width // gb
    summed = jnp.concatenate(sums, axis=1)
    bit = 1
    while bit < rows:
        summed = summed + swap(summed, "row", bit)
        bit *= 2

    point_density = summed[0]
    gradient = 2.0 * summed[1:]
    squared = jnp.sum(gradient * gradient, axis=0)
    atoms = atom_factor.shape[0]
    chooser = (atom_of_block[:, None] == jnp.arange(atoms, dtype=jnp.int32)[None, :]).astype(F32)
    block_factor = jnp.dot(chooser, atom_factor, precision=lax.Precision.HIGHEST)
    group_size = points // atom_of_block.shape[0]
    weights = (quad_weight.reshape(-1, group_size) * block_factor[:, None]).reshape(
        points
    ) / math.sqrt(points * cols)
    density_pot, gradient_pot = potentials(point_density, squared, core_density)
    scalar_part = 0.5 * weights * density_pot
    vector_part = 2.0 * weights * gradient_pot * gradient
    parts = jnp.concatenate([scalar_part[None], vector_part], axis=0)
    half = call(
        functools.partial(half_kernel, sb, gb), shape((row_count, points), BF16),
        [SCALARS, WHOLE, WHOLE], 8 * basis_values.size, 2 * basis_values.size,
    )(screen, basis_values, parts)

    beyond = (beside, *near, *far, *across)
    product = 2 * row_count * points * share * count
    mirrored_other = call(
        functools.partial(mirrored_other_kernel, share, count, chunks),
        shape((REACH, count, share, row_count)), [WHOLE] * (1 + len(beyond)),
        product * 2, 4 * row_count * points,
    )(half, *beyond)
    mirrored_found = swap(mirrored_other, "col", 1)
    direct_other = call(
        functools.partial(direct_other_kernel, share, count, chunks),
        shape((REACH + 1, count, share, row_count)),
        [WHOLE] * 2 + [ANYWHERE] + [WHOLE] * len(beyond),
        product * 4, 6 * row_count * points,
    )(half, own, mirrored_other, *beyond)
    direct_found = swap(direct_other, "col", 1)
    kept = count // 2
    mirrored_keep, mirrored_send = call(
        functools.partial(mirrored_own_kernel, share, count, chunks),
        [
            shape((REACH, kept, share, row_count)),
            shape((REACH, kept, share, row_count), BF16),
        ],
        [WHOLE] * (2 + len(beyond)), product * 2, 6 * row_count * points,
    )(half, mirrored_found, *beyond)
    spare = max(share, 128)
    direct_keep, direct_send = call(
        functools.partial(direct_own_kernel, share, count, chunks),
        [
            shape((REACH + 1, kept, share, row_count)),
            shape((kept, share, 3 * row_count + spare), BF16),
        ],
        [WHOLE] * 2 + [ANYWHERE] + [WHOLE] * (1 + len(beyond)), product * 4, 8 * row_count * points,
    )(half, own, mirrored_keep, direct_found, *beyond)

    def scatter(total, axis):
        bit = 4
        while bit < cols:
            paired = total.reshape(*total.shape[:axis], -1, 2, *total.shape[axis + 1 :])
            mine = (col // bit) % 2
            keep = lax.dynamic_index_in_dim(paired, mine, axis + 1, keepdims=False)
            send = lax.dynamic_index_in_dim(paired, 1 - mine, axis + 1, keepdims=False)
            total = keep + swap(send, "col", bit)
            bit *= 2
        return total

    found = swap(mirrored_send, "col", 2)
    mirrored = mirrored_keep + found.astype(F32)
    mirrored = scatter(mirrored, 1).astype(BF16)
    mirrored = [from_ahead(mirrored[k, 0], k + 1) for k in range(REACH)]
    found = swap(direct_send, "col", 2)
    if kept > 1:
        total = call(
            functools.partial(joined_kernel, share), shape((kept, share, 3 * row_count)),
            [WHOLE] * 2, direct_keep.size, 8 * direct_keep.size,
        )(direct_keep, found)
        total = scatter(total, 0)[0]
        zero = jnp.zeros((share, row_count), BF16)
        return total + jnp.concatenate([zero, *mirrored], axis=1).astype(F32)
    return call(
        functools.partial(final_kernel, share), shape((1, share, 3 * row_count)),
        [WHOLE] * (2 + REACH), direct_keep.size, 10 * direct_keep.size,
    )(direct_keep, found, *mirrored)[0]


def solution(mesh):
    in_specs = (
        P(None, "row", "col"),
        P("row", None),
        P("row", "col"),
        P("col"),
        P(),
        P("col"),
        P("col"),
    )
    out_specs = P(("row", "col"), None)

    return jax.shard_map(body, mesh=mesh, in_specs=in_specs, out_specs=out_specs, check_vma=False)
```

```python
import functools
import math

import jax
import jax.numpy as jnp
from jax import lax
from jax.experimental import pallas as pl
from jax.experimental.pallas import tpu as pltpu
from jax.sharding import PartitionSpec as P


BAND = 5
REACH = BAND // 2

KAPPA_VALUE = 0.804
MU_VALUE = 0.22
SLATER_COEF = 0.7386


WHOLE = pl.BlockSpec(memory_space=pltpu.VMEM)
SCALARS = pl.BlockSpec(memory_space=pltpu.SMEM)
ANYWHERE = pl.BlockSpec(memory_space=pl.ANY)
PARAMS = pltpu.CompilerParams(vmem_limit_bytes=20 << 20)
F32 = jnp.float32
BF16 = jnp.bfloat16


def from_ahead(block, distance):
    size = lax.axis_size("row")
    return lax.ppermute(block, "row", [((i + distance) % size, i) for i in range(size)])


def from_side(block, distance):
    size = lax.axis_size("row")
    route = [((i + (distance if i % 2 == 0 else -distance)) % size, i) for i in range(size)]
    return lax.ppermute(block, "row", route)


def swap(block, axis, bit):
    return lax.ppermute(block, axis, [(i, i ^ bit) for i in range(lax.axis_size(axis))])


def energy_density(density_in, squared_in, core):
    regular = jnp.sqrt(density_in * density_in + core * core)
    reduced = squared_in * regular ** (-8.0 / 3.0)
    enhance = 1.0 + KAPPA_VALUE - KAPPA_VALUE / (1.0 + MU_VALUE * reduced / KAPPA_VALUE)
    return -SLATER_COEF * regular ** (4.0 / 3.0) * enhance


def potentials(density_in, squared_in, core):

    def total_energy(first_arg, second_arg):
        return jnp.sum(energy_density(first_arg, second_arg, core))

    return jax.grad(total_energy, argnums=(0, 1))(density_in, squared_in)


def call(kernel, outs, in_specs, flops, bytes_accessed, out_specs=None, scratch=()):
    return pl.pallas_call(
        kernel,
        out_shape=outs,
        in_specs=in_specs,
        out_specs=jax.tree.map(lambda _: WHOLE, outs) if out_specs is None else out_specs,
        scratch_shapes=list(scratch),
        compiler_params=PARAMS,
        cost_estimate=pl.CostEstimate(
            flops=int(flops), bytes_accessed=int(bytes_accessed), transcendentals=0
        ),
    )


def dot(left, right):
    return jnp.dot(left, right, preferred_element_type=F32)


def dot_rows(left, right):
    return lax.dot_general(left, right, (((1,), (1,)), ((), ())), preferred_element_type=F32)


def position():
    col = lax.axis_index("col")
    return lax.axis_index("row") % 2, col % 2, (col // 2) % 2


def mask_kernel(sb, gb, screen_ref, basis_ref, own_ref, *rest):
    chunk_refs, (tile_ref, sems) = rest[:-2], rest[-2:]
    row_count, _ = own_ref.shape
    copies = []
    for row in range(row_count // sb):
        window = pl.ds(row * sb, sb)
        copy = pltpu.make_async_copy(basis_ref.at[0, window], tile_ref.at[window], sems.at[row])
        copy.start()
        copies.append(copy)
    for row, copy in enumerate(copies):
        rows = slice(row * sb, (row + 1) * sb)
        copy.wait()
        col = 0
        for chunk in chunk_refs:
            for start in range(0, chunk.shape[1], gb):
                keep = screen_ref[row, col // gb].astype(F32)
                tile = (tile_ref[rows, col : col + gb].astype(F32) * keep).astype(BF16)
                own_ref[rows, col : col + gb] = tile
                chunk[rows, start : start + gb] = tile
                col += gb


def split_kernel(density_ref, high_ref, low_ref):
    size = density_ref.shape[0]
    for column in range(BAND):
        strip = density_ref[:, column * size : (column + 1) * size]
        high = strip.astype(BF16)
        high_ref[column] = high
        low_ref[column] = (strip - high.astype(F32)).astype(BF16)


def both(high_ref, low_ref, column, block):
    return dot(high_ref[column], block) + dot(low_ref[column], block)


def early_kernel(start, high_ref, low_ref, own, beside, near, total_ref):
    sign = 1 - 2 * position()[0]
    cols = slice(start, start + near.shape[1])
    total_ref[...] = (
        both(high_ref, low_ref, REACH, own[:, cols])
        + both(high_ref, low_ref, REACH + sign, beside[:, cols])
        + both(high_ref, low_ref, REACH + 2 * sign, near[...])
    )


def sums_kernel(sb, gb, first, screen_ref, high_ref, low_ref, partial_ref, far, across, basis_ref,
                sums_ref, total_ref):
    sign = 1 - 2 * position()[0]
    total_ref[...] = (
        partial_ref[...]
        + both(high_ref, low_ref, REACH - 2 * sign, far[...])
        + both(high_ref, low_ref, REACH - sign, across[...])
    )
    components, row_count, width = basis_ref.shape[0], far.shape[0], far.shape[1]
    for part in range(width // gb):
        cols = slice(part * gb, (part + 1) * gb)
        source = slice((first + part) * gb, (first + part + 1) * gb)
        found = [jnp.zeros((1, gb), F32) for _ in range(components)]
        for row in range(row_count // sb):
            rows = slice(row * sb, (row + 1) * sb)
            keep = screen_ref[row, first + part].astype(F32)
            applied = total_ref[rows, cols]
            for c in range(components):
                product = basis_ref[c, rows, source].astype(F32) * applied
                found[c] += keep * jnp.sum(product, axis=0, keepdims=True)
        for c in range(components):
            sums_ref[c : c + 1, cols] = found[c]


def half_kernel(sb, gb, screen_ref, basis_ref, parts_ref, half_ref):
    components, row_count, points = basis_ref.shape
    for part in range(points // gb):
        cols = slice(part * gb, (part + 1) * gb)
        for row in range(row_count // sb):
            rows = slice(row * sb, (row + 1) * sb)
            keep = screen_ref[row, part].astype(F32)
            total = (parts_ref[0:1, cols] * keep) * basis_ref[0, rows, cols].astype(F32)
            for c in range(1, components):
                total += (parts_ref[c : c + 1, cols] * keep) * basis_ref[c, rows, cols].astype(F32)
            half_ref[rows, cols] = total.astype(BF16)


def rows_of(ref, cols, side, share, count):
    blocks = []
    for step in range(count):
        window = pl.ds(pl.multiple_of((2 * step + side) * share, share), share)
        blocks.append(ref[window, cols])
    return jnp.concatenate(blocks, axis=0) if count > 1 else blocks[0]


def pieces(blocks):
    start = 0
    for block in blocks:
        width = block.shape[1]
        yield slice(start, start + width), block
        start += width


def mirrored_product(half_ref, blocks, side, share, count):
    total = 0
    for cols, block in pieces(blocks):
        left = rows_of(block, slice(None), side, share, count)
        total += dot_rows(left, half_ref[:, cols])
    return total.reshape(count, share, half_ref.shape[0])


def central_product(half_ref, own, side, share, count):
    cols = slice(None)
    total = dot_rows(rows_of(own, cols, side, share, count), half_ref[...])
    total += dot_rows(rows_of(half_ref, cols, side, share, count), own[...])
    return total.reshape(count, share, half_ref.shape[0])


def direct_product(half_ref, blocks, side, share, count):
    total = 0
    for cols, block in pieces(blocks):
        total += dot_rows(rows_of(half_ref, cols, side, share, count), block[...])
    return total.reshape(count, share, half_ref.shape[0])


def neighbours(refs, chunks):
    beside, near = refs[:1], refs[1 : 1 + chunks]
    far, across = refs[1 + chunks : 1 + 2 * chunks], refs[1 + 2 * chunks : 1 + 3 * chunks]
    return (beside, near), (across, far)


def behind(first, second, run):
    odd = position()[0]

    @pl.when(odd != 0)
    def _():
        run(first)

    @pl.when(odd == 0)
    def _():
        run(second)


def on_side(refs, chunks, ahead, run):
    first, second = neighbours(refs, chunks)
    odd = position()[0]

    @pl.when(odd == (0 if ahead else 1))
    def _():
        run(*first)

    @pl.when(odd == (1 if ahead else 0))
    def _():
        run(*second)


def deposit(total, side, keep_ref, send_ref):
    for step in range(total.shape[-3] // 2):
        low, high = total[..., 2 * step, :, :], total[..., 2 * step + 1, :, :]
        keep_ref[..., step, :, :] = jnp.where(side == 0, low, high)
        send_ref[..., step, :, :] = jnp.where(side == 0, high, low).astype(send_ref.dtype)


def mirrored_other_kernel(share, count, cut, half_ref, earlier_ref, *refs):
    first, second, out = refs[:cut], refs[cut:-1], refs[-1]
    side = 1 - position()[1]

    def run(blocks):
        out[...] = mirrored_product(half_ref, blocks, side, share, count)

    behind(first, second, run)


def mirrored_own_kernel(share, count, cut, half_ref, found_ref, *refs):
    first, second, keep_ref, send_ref = refs[:cut], refs[cut:-2], refs[-2], refs[-1]
    _, core, side = position()

    def run(blocks):
        total = mirrored_product(half_ref, blocks, core, share, count)
        deposit(total + found_ref[...], side, keep_ref, send_ref)

    behind(first, second, run)


def central_other_kernel(share, count, half_ref, own, out):
    out[...] = central_product(half_ref, own, 1 - position()[1], share, count)


def direct_other_kernel(share, count, chunks, half_ref, earlier_ref, *refs):
    refs, out = refs[:-1], refs[-1]
    side = 1 - position()[1]

    def run(one, two):
        out[0] = direct_product(half_ref, one, side, share, count)
        out[1] = direct_product(half_ref, two, side, share, count)

    on_side(refs, chunks, True, run)


def central_own_kernel(share, count, half_ref, own, found_ref, keep_ref, send_ref):
    _, core, side = position()
    size = half_ref.shape[0]
    spare = send_ref.shape[-1] - size
    total = central_product(half_ref, own, core, share, count) + found_ref[...]
    for step in range(count // 2):
        low, high = total[2 * step], total[2 * step + 1]
        keep_ref[step] = jnp.where(side == 0, low, high)
        send = jnp.where(side == 0, high, low)
        rounded = send.astype(BF16)
        send_ref[step, :, :size] = rounded
        quarter = (2 * step + 1 - side) * 2 + core
        for block in range(size // spare):

            @pl.when((quarter * share) // spare == block)
            def _():
                cols = slice(block * spare, (block + 1) * spare)
                rest = send[:, cols] - rounded[:, cols].astype(F32)
                send_ref[step, :, size:] = rest.astype(BF16)


def direct_own_kernel(share, count, chunks, half_ref, found_ref, earlier_ref, *refs):
    refs, keep_ref, send_ref = refs[:-2], refs[-2], refs[-1]
    _, core, side = position()

    def run(one, two):
        for k, blocks in enumerate((one, two)):
            total = direct_product(half_ref, blocks, core, share, count) + found_ref[k]
            deposit(total, side, keep_ref.at[k], send_ref.at[k])

    on_side(refs, chunks, True, run)


def joined_kernel(share, central_ref, found_ref, keep_ref, direct_ref, out_ref):
    _, core, side = position()
    size = keep_ref.shape[-1]
    spare = found_ref.shape[-1] - size
    for step in range(found_ref.shape[0]):
        out_ref[step, :, :size] = central_ref[step] + found_ref[step, :, :size].astype(F32)
        for k in range(REACH):
            cols = slice((k + 1) * size, (k + 2) * size)
            out_ref[step, :, cols] = keep_ref[k, step] + direct_ref[k, step].astype(F32)
        quarter = (2 * step + side) * 2 + core
        for block in range(size // spare):

            @pl.when((quarter * share) // spare == block)
            def _():
                cols = slice(block * spare, (block + 1) * spare)
                out_ref[step, :, cols] += found_ref[step, :, size:].astype(F32)


def final_kernel(share, central_ref, found_ref, keep_ref, direct_ref, *refs):
    mirrored, out_ref = refs[:-1], refs[-1]
    joined_kernel(share, central_ref, found_ref, keep_ref, direct_ref, out_ref)
    size = keep_ref.shape[-1]
    for k, block in enumerate(mirrored):
        cols = slice((k + 1) * size, (k + 2) * size)
        out_ref[0, :, cols] += block[...].astype(F32)


def shape(dims, kind=F32):
    return jax.ShapeDtypeStruct(dims, kind)


def body(basis_values, density, screen, atom_of_block, atom_factor, quad_weight, core_density):
    rows, cols = lax.axis_size("row"), lax.axis_size("col")
    col = lax.axis_index("col")
    components, row_count, points = basis_values.shape
    sb, gb = row_count // screen.shape[0], points // screen.shape[1]
    eighth = max(1, screen.shape[1] // 8) * gb
    widths = (points - 3 * eighth, 2 * eighth, eighth)
    chunks = len(widths)
    share, count = row_count // cols, cols // 2
    square = 2 * row_count * row_count

    own, *mine = call(
        functools.partial(mask_kernel, sb, gb),
        [shape((row_count, width), BF16) for width in (points, *widths)],
        [SCALARS, pl.BlockSpec(memory_space=pltpu.HBM)], row_count * points, 6 * row_count * points,
        scratch=[
            pltpu.VMEM((row_count, points), BF16),
            pltpu.SemaphoreType.DMA((screen.shape[0],)),
        ],
    )(screen, pltpu.with_memory_space_constraint(basis_values, pltpu.HBM))
    near, far, across = [], [], []
    for chunk, block in enumerate(mine):
        near.append(from_side(block, 2))
        far.append(from_side(block, -2))
        across.append(swap(near[chunk], "row", 1))
    beside = swap(own, "row", 1)

    high, low = call(
        split_kernel, [shape((BAND, row_count, row_count), BF16)] * 2, [WHOLE],
        density.size * 4, density.size * 8,
    )(density)
    sums, first = [], 0
    for chunk, width in enumerate(widths):
        partial = call(
            functools.partial(early_kernel, first), shape((row_count, width)), [WHOLE] * 5,
            6 * square * width, 10 * square,
        )(high, low, own, beside, near[chunk])
        found = call(
            functools.partial(sums_kernel, sb, gb, first // gb), shape((components, width)),
            [SCALARS] + [WHOLE] * 6, 4 * square * width, 6 * square,
            scratch=[pltpu.VMEM((row_count, width), F32)],
        )(screen, high, low, partial, far[chunk], across[chunk], basis_values)
        sums.append(found)
        first += width
    summed = jnp.concatenate(sums, axis=1)
    bit = 1
    while bit < rows:
        summed = summed + swap(summed, "row", bit)
        bit *= 2

    point_density = summed[0]
    gradient = 2.0 * summed[1:]
    squared = jnp.sum(gradient * gradient, axis=0)
    atoms = atom_factor.shape[0]
    chooser = (atom_of_block[:, None] == jnp.arange(atoms, dtype=jnp.int32)[None, :]).astype(F32)
    block_factor = jnp.dot(chooser, atom_factor, precision=lax.Precision.HIGHEST)
    group_size = points // atom_of_block.shape[0]
    weights = (quad_weight.reshape(-1, group_size) * block_factor[:, None]).reshape(
        points
    ) / math.sqrt(points * cols)
    density_pot, gradient_pot = potentials(point_density, squared, core_density)
    scalar_part = 0.5 * weights * density_pot
    vector_part = 2.0 * weights * gradient_pot * gradient
    parts = jnp.concatenate([scalar_part[None], vector_part], axis=0)
    half = call(
        functools.partial(half_kernel, sb, gb), shape((row_count, points), BF16),
        [SCALARS, WHOLE, WHOLE], 8 * basis_values.size, 2 * basis_values.size,
    )(screen, basis_values, parts)

    beyond = (beside, *near, *far, *across)
    paired = {1: ((beside,), across), 2: (near, far)}
    product = 2 * row_count * points * share * count
    kept = count // 2
    block = (count, share, row_count)
    mirrored_found, earlier = {}, half
    for k in (2, 1):
        first, second = paired[k]
        earlier = call(
            functools.partial(mirrored_other_kernel, share, count, len(first)), shape(block),
            [WHOLE, ANYWHERE] + [WHOLE] * len((*first, *second)), product, 3 * half.size,
        )(half, earlier, *first, *second)
        mirrored_found[k] = swap(earlier, "col", 1)
    central_other = call(
        functools.partial(central_other_kernel, share, count), shape(block),
        [WHOLE] * 2, 2 * product, 4 * half.size,
    )(half, own)
    central_found = swap(central_other, "col", 1)
    mirrored_keep, mirrored_send = {}, {}
    for k in (2, 1):
        first, second = paired[k]
        mirrored_keep[k], mirrored_send[k] = call(
            functools.partial(mirrored_own_kernel, share, count, len(first)),
            [shape((kept, share, row_count)), shape((kept, share, row_count), BF16)],
            [WHOLE] * len((half, half, *first, *second)), product, 4 * half.size,
        )(half, mirrored_found[k], *first, *second)
    direct_other = call(
        functools.partial(direct_other_kernel, share, count, chunks), shape((REACH, *block)),
        [WHOLE, ANYWHERE] + [WHOLE] * len(beyond), product * 2, 4 * half.size,
    )(half, central_other, *beyond)
    direct_found = swap(direct_other, "col", 1)
    spare = max(share, 128)
    central_keep, central_send = call(
        functools.partial(central_own_kernel, share, count),
        [
            shape((kept, share, row_count)),
            shape((kept, share, row_count + spare), BF16),
        ],
        [WHOLE] * 3, product * 2, 4 * half.size,
    )(half, own, central_found)
    central_found = swap(central_send, "col", 2)
    direct_keep, direct_send = call(
        functools.partial(direct_own_kernel, share, count, chunks),
        [
            shape((REACH, kept, share, row_count)),
            shape((REACH, kept, share, row_count), BF16),
        ],
        [WHOLE] * 2 + [ANYWHERE] + [WHOLE] * len(beyond), product * 2, 4 * half.size,
    )(half, direct_found, central_keep, *beyond)

    def scatter(total, axis):
        bit = 4
        while bit < cols:
            paired = total.reshape(*total.shape[:axis], -1, 2, *total.shape[axis + 1 :])
            mine = (col // bit) % 2
            keep = lax.dynamic_index_in_dim(paired, mine, axis + 1, keepdims=False)
            send = lax.dynamic_index_in_dim(paired, 1 - mine, axis + 1, keepdims=False)
            total = keep + swap(send, "col", bit)
            bit *= 2
        return total

    mirrored = []
    for k in (2, 1):
        found = swap(mirrored_send[k], "col", 2)
        total = scatter(mirrored_keep[k] + found.astype(F32), 0).astype(BF16)
        mirrored.insert(0, from_ahead(total[0], k))
    found = swap(direct_send, "col", 2)
    partial = (central_keep, central_found, direct_keep, found)
    if kept > 1:
        total = call(
            functools.partial(joined_kernel, share), shape((kept, share, 3 * row_count)),
            [WHOLE] * 4, direct_keep.size, 8 * direct_keep.size,
        )(*partial)
        total = scatter(total, 0)[0]
        zero = jnp.zeros((share, row_count), BF16)
        return total + jnp.concatenate([zero, *mirrored], axis=1).astype(F32)
    return call(
        functools.partial(final_kernel, share), shape((1, share, 3 * row_count)),
        [WHOLE] * (4 + REACH), direct_keep.size, 10 * direct_keep.size,
    )(*partial, *mirrored)[0]


def solution(mesh):
    in_specs = (
        P(None, "row", "col"),
        P("row", None),
        P("row", "col"),
        P("col"),
        P(),
        P("col"),
        P("col"),
    )
    out_specs = P(("row", "col"), None)

    return jax.shard_map(body, mesh=mesh, in_specs=in_specs, out_specs=out_specs, check_vma=False)
```

```python
import functools
import math

import jax
import jax.numpy as jnp
from jax import lax
from jax.experimental import pallas as pl
from jax.experimental.pallas import tpu as pltpu
from jax.sharding import PartitionSpec as P


BAND = 5
REACH = BAND // 2

KAPPA_VALUE = 0.804
MU_VALUE = 0.22
SLATER_COEF = 0.7386


WHOLE = pl.BlockSpec(memory_space=pltpu.VMEM)
SCALARS = pl.BlockSpec(memory_space=pltpu.SMEM)
ANYWHERE = pl.BlockSpec(memory_space=pl.ANY)
PARAMS = pltpu.CompilerParams(vmem_limit_bytes=20 << 20)
F32 = jnp.float32
BF16 = jnp.bfloat16


def from_ahead(block, distance):
    size = lax.axis_size("row")
    return lax.ppermute(block, "row", [((i + distance) % size, i) for i in range(size)])


def from_side(block, distance):
    size = lax.axis_size("row")
    route = [((i + (distance if i % 2 == 0 else -distance)) % size, i) for i in range(size)]
    return lax.ppermute(block, "row", route)


def swap(block, axis, bit):
    return lax.ppermute(block, axis, [(i, i ^ bit) for i in range(lax.axis_size(axis))])


def energy_density(density_in, squared_in, core):
    regular = jnp.sqrt(density_in * density_in + core * core)
    reduced = squared_in * regular ** (-8.0 / 3.0)
    enhance = 1.0 + KAPPA_VALUE - KAPPA_VALUE / (1.0 + MU_VALUE * reduced / KAPPA_VALUE)
    return -SLATER_COEF * regular ** (4.0 / 3.0) * enhance


def potentials(density_in, squared_in, core):

    def total_energy(first_arg, second_arg):
        return jnp.sum(energy_density(first_arg, second_arg, core))

    return jax.grad(total_energy, argnums=(0, 1))(density_in, squared_in)


def call(kernel, outs, in_specs, flops, bytes_accessed, out_specs=None, scratch=()):
    return pl.pallas_call(
        kernel,
        out_shape=outs,
        in_specs=in_specs,
        out_specs=jax.tree.map(lambda _: WHOLE, outs) if out_specs is None else out_specs,
        scratch_shapes=list(scratch),
        compiler_params=PARAMS,
        cost_estimate=pl.CostEstimate(
            flops=int(flops), bytes_accessed=int(bytes_accessed), transcendentals=0
        ),
    )


def dot(left, right):
    return jnp.dot(left, right, preferred_element_type=F32)


def dot_rows(left, right):
    return lax.dot_general(left, right, (((1,), (1,)), ((), ())), preferred_element_type=F32)


def position():
    col = lax.axis_index("col")
    return lax.axis_index("row") % 2, col % 2, (col // 2) % 2


def mask_kernel(sb, gb, screen_hbm, basis_ref, own_ref, *rest):
    chunk_refs, (screen_ref, tile_ref, sem, sems) = rest[:-4], rest[-4:]
    row_count, _ = own_ref.shape
    screen_copy = pltpu.make_async_copy(screen_hbm, screen_ref, sem)
    screen_copy.start()
    copies = []
    for row in range(row_count // sb):
        window = pl.ds(row * sb, sb)
        copy = pltpu.make_async_copy(basis_ref.at[0, window], tile_ref.at[window], sems.at[row])
        copy.start()
        copies.append(copy)
    screen_copy.wait()
    for row, copy in enumerate(copies):
        rows = slice(row * sb, (row + 1) * sb)
        copy.wait()
        col = 0
        for chunk in chunk_refs:
            for start in range(0, chunk.shape[1], gb):
                keep = screen_ref[row, col // gb].astype(F32)
                tile = (tile_ref[rows, col : col + gb].astype(F32) * keep).astype(BF16)
                own_ref[rows, col : col + gb] = tile
                chunk[rows, start : start + gb] = tile
                col += gb


def split_kernel(density_ref, high_ref, low_ref):
    size = density_ref.shape[0]
    for column in range(BAND):
        strip = density_ref[:, column * size : (column + 1) * size]
        high = strip.astype(BF16)
        high_ref[column] = high
        low_ref[column] = (strip - high.astype(F32)).astype(BF16)


def both(high_ref, low_ref, column, block):
    return dot(high_ref[column], block) + dot(low_ref[column], block)


def early_kernel(start, high_ref, low_ref, own, beside, near, total_ref):
    sign = 1 - 2 * position()[0]
    cols = slice(start, start + near.shape[1])
    total_ref[...] = (
        both(high_ref, low_ref, REACH, own[:, cols])
        + both(high_ref, low_ref, REACH + sign, beside[:, cols])
        + both(high_ref, low_ref, REACH + 2 * sign, near[...])
    )


def later_kernel(high_ref, low_ref, partial_ref, across, total_ref):
    sign = 1 - 2 * position()[0]
    total_ref[...] = partial_ref[...] + both(high_ref, low_ref, REACH - sign, across[...])


def sums_kernel(start, high_ref, low_ref, partial_ref, far, masked_ref, sums_ref, total_ref):
    sign = 1 - 2 * position()[0]
    width = far.shape[1]
    total_ref[...] = partial_ref[...] + both(high_ref, low_ref, REACH - 2 * sign, far[...])
    for c in range(masked_ref.shape[0]):
        product = masked_ref[c, :, start : start + width] * total_ref[...]
        sums_ref[c : c + 1, :] = jnp.sum(product, axis=0, keepdims=True)


def widen_kernel(sb, gb, screen_ref, basis_ref, masked_ref):
    components, row_count, points = basis_ref.shape
    for part in range(points // gb):
        cols = slice(part * gb, (part + 1) * gb)
        for row in range(row_count // sb):
            rows = slice(row * sb, (row + 1) * sb)
            keep = screen_ref[row, part].astype(F32)
            for c in range(components):
                masked_ref[c, rows, cols] = basis_ref[c, rows, cols].astype(F32) * keep


def half_kernel(masked_ref, parts_ref, half_ref):
    components, row_count, points = masked_ref.shape
    for start in range(0, points, 128):
        cols = slice(start, start + 128)
        for row in range(0, row_count, 128):
            rows = slice(row, row + 128)
            total = parts_ref[0:1, cols] * masked_ref[0, rows, cols]
            for c in range(1, components):
                total += parts_ref[c : c + 1, cols] * masked_ref[c, rows, cols]
            half_ref[rows, cols] = total.astype(BF16)


def sorted_kernel(chunks, beside, *refs):
    near, far, across = (refs[i * chunks : (i + 1) * chunks] for i in range(3))
    ahead_ref, behind_ref = refs[3 * chunks :]

    def fill(here_ref, there_ref):
        here_ref[0] = beside[...]
        start = 0
        for one, two, three in zip(near, across, far):
            cols = slice(start, start + one.shape[1])
            here_ref[1, :, cols] = one[...]
            there_ref[0, :, cols] = two[...]
            there_ref[1, :, cols] = three[...]
            start += one.shape[1]

    odd = position()[0]

    @pl.when(odd == 0)
    def _():
        fill(ahead_ref, behind_ref)

    @pl.when(odd != 0)
    def _():
        fill(behind_ref, ahead_ref)


def rows_of(ref, side, share, count):
    blocks = []
    for step in range(count):
        window = pl.ds(pl.multiple_of((2 * step + side) * share, share), share)
        blocks.append(ref[window, :])
    return jnp.concatenate(blocks, axis=0) if count > 1 else blocks[0]


def mirrored_product(half_ref, block, side, share, count):
    total = dot_rows(rows_of(block, side, share, count), half_ref[...])
    return total.reshape(count, share, half_ref.shape[0])


def central_product(half_ref, own, side, share, count):
    total = dot_rows(rows_of(own, side, share, count), half_ref[...])
    total += dot_rows(rows_of(half_ref, side, share, count), own[...])
    return total.reshape(count, share, half_ref.shape[0])


def direct_product(half_ref, block, side, share, count):
    total = dot_rows(rows_of(half_ref, side, share, count), block[...])
    return total.reshape(count, share, half_ref.shape[0])


def deposit(total, side, keep_ref, send_ref):
    for step in range(total.shape[-3] // 2):
        low, high = total[..., 2 * step, :, :], total[..., 2 * step + 1, :, :]
        keep_ref[..., step, :, :] = jnp.where(side == 0, low, high)
        send_ref[..., step, :, :] = jnp.where(side == 0, high, low).astype(send_ref.dtype)


def mirrored_other_kernel(share, count, k, half_ref, earlier_ref, behind_ref, out):
    side = 1 - position()[1]
    out[...] = mirrored_product(half_ref, behind_ref.at[k], side, share, count)


def mirrored_own_kernel(share, count, k, half_ref, found_ref, behind_ref, keep_ref, send_ref):
    _, core, side = position()
    total = mirrored_product(half_ref, behind_ref.at[k], core, share, count)
    deposit(total + found_ref[...], side, keep_ref, send_ref)


def central_other_kernel(share, count, half_ref, own, earlier_ref, out):
    out[...] = central_product(half_ref, own, 1 - position()[1], share, count)


def direct_other_kernel(share, count, half_ref, earlier_ref, ahead_ref, out):
    side = 1 - position()[1]
    for k in range(REACH):
        out[k] = direct_product(half_ref, ahead_ref.at[k], side, share, count)


def central_own_kernel(share, count, half_ref, own, found_ref, keep_ref, send_ref):
    _, core, side = position()
    size = half_ref.shape[0]
    spare = send_ref.shape[-1] - size
    total = central_product(half_ref, own, core, share, count) + found_ref[...]
    for step in range(count // 2):
        low, high = total[2 * step], total[2 * step + 1]
        keep_ref[step] = jnp.where(side == 0, low, high)
        send = jnp.where(side == 0, high, low)
        rounded = send.astype(BF16)
        send_ref[step, :, :size] = rounded
        quarter = (2 * step + 1 - side) * 2 + core
        for block in range(size // spare):

            @pl.when((quarter * share) // spare == block)
            def _():
                cols = slice(block * spare, (block + 1) * spare)
                rest = send[:, cols] - rounded[:, cols].astype(F32)
                send_ref[step, :, size:] = rest.astype(BF16)


def direct_own_kernel(share, count, half_ref, found_ref, earlier_ref, ahead_ref, keep_ref, send_ref):
    _, core, side = position()
    for k in range(REACH):
        total = direct_product(half_ref, ahead_ref.at[k], core, share, count) + found_ref[k]
        deposit(total, side, keep_ref.at[k], send_ref.at[k])


def joined_kernel(share, central_ref, found_ref, keep_ref, direct_ref, out_ref):
    _, core, side = position()
    size = keep_ref.shape[-1]
    spare = found_ref.shape[-1] - size
    for step in range(found_ref.shape[0]):
        out_ref[step, :, :size] = central_ref[step] + found_ref[step, :, :size].astype(F32)
        for k in range(REACH):
            cols = slice((k + 1) * size, (k + 2) * size)
            out_ref[step, :, cols] = keep_ref[k, step] + direct_ref[k, step].astype(F32)
        quarter = (2 * step + side) * 2 + core
        for block in range(size // spare):

            @pl.when((quarter * share) // spare == block)
            def _():
                cols = slice(block * spare, (block + 1) * spare)
                out_ref[step, :, cols] += found_ref[step, :, size:].astype(F32)


def final_kernel(share, central_ref, found_ref, keep_ref, direct_ref, *refs):
    mirrored, out_ref = refs[:-1], refs[-1]
    joined_kernel(share, central_ref, found_ref, keep_ref, direct_ref, out_ref)
    size = keep_ref.shape[-1]
    for k, block in enumerate(mirrored):
        cols = slice((k + 1) * size, (k + 2) * size)
        out_ref[0, :, cols] += block[...].astype(F32)


def shape(dims, kind=F32):
    return jax.ShapeDtypeStruct(dims, kind)


def body(basis_values, density, screen, atom_of_block, atom_factor, quad_weight, core_density):
    rows, cols = lax.axis_size("row"), lax.axis_size("col")
    col = lax.axis_index("col")
    components, row_count, points = basis_values.shape
    sb, gb = row_count // screen.shape[0], points // screen.shape[1]
    eighth = max(1, screen.shape[1] // 8) * gb
    widths = (points - 3 * eighth, 2 * eighth, eighth)
    chunks = len(widths)
    share, count = row_count // cols, cols // 2
    square = 2 * row_count * row_count

    own, *mine = call(
        functools.partial(mask_kernel, sb, gb),
        [shape((row_count, width), BF16) for width in (points, *widths)],
        [pl.BlockSpec(memory_space=pltpu.HBM)] * 2, row_count * points, 6 * row_count * points,
        scratch=[
            pltpu.SMEM(screen.shape, jnp.int32),
            pltpu.VMEM((row_count, points), BF16),
            pltpu.SemaphoreType.DMA,
            pltpu.SemaphoreType.DMA((screen.shape[0],)),
        ],
    )(pltpu.with_memory_space_constraint(screen, pltpu.HBM), pltpu.with_memory_space_constraint(basis_values, pltpu.HBM))
    near, far, across = [], [], []
    for chunk, block in enumerate(mine):
        near.append(from_side(block, 2))
        far.append(from_side(block, -2))
        across.append(swap(near[chunk], "row", 1))
    beside = swap(own, "row", 1)

    high, low = call(
        split_kernel, [shape((BAND, row_count, row_count), BF16)] * 2, [WHOLE],
        density.size * 4, density.size * 8,
    )(density)
    masked = call(
        functools.partial(widen_kernel, sb, gb), shape(basis_values.shape), [SCALARS, WHOLE],
        basis_values.size, 6 * basis_values.size,
    )(screen, basis_values)
    sums, first = [], 0
    for chunk, width in enumerate(widths):
        total = shape((row_count, width))
        partial = call(
            functools.partial(early_kernel, first), total, [WHOLE] * 5,
            6 * square * width, 10 * square,
        )(high, low, own, beside, near[chunk])
        partial = call(later_kernel, total, [WHOLE] * 4, 2 * square * width, 4 * square)(
            high, low, partial, across[chunk]
        )
        found = call(
            functools.partial(sums_kernel, first), shape((components, width)),
            [WHOLE] * 5, 2 * square * width, 6 * square,
            scratch=[pltpu.VMEM((row_count, width), F32)],
        )(high, low, partial, far[chunk], masked)
        sums.append(found)
        first += width
    ahead, behind = call(
        functools.partial(sorted_kernel, chunks),
        [shape((REACH, row_count, points), BF16)] * 2, [WHOLE] * (1 + 3 * chunks),
        row_count * points, 16 * row_count * points,
    )(beside, *near, *far, *across)
    summed = jnp.concatenate(sums, axis=1)
    bit = 1
    while bit < rows:
        found = swap(summed, "row", bit)
        summed = summed + found
        bit *= 2

    point_density = summed[0]
    gradient = 2.0 * summed[1:]
    squared = jnp.sum(gradient * gradient, axis=0)
    atoms = atom_factor.shape[0]
    chooser = (atom_of_block[:, None] == jnp.arange(atoms, dtype=jnp.int32)[None, :]).astype(F32)
    block_factor = jnp.dot(chooser, atom_factor, precision=lax.Precision.HIGHEST)
    group_size = points // atom_of_block.shape[0]
    weights = (quad_weight.reshape(-1, group_size) * block_factor[:, None]).reshape(
        points
    ) / math.sqrt(points * cols)
    density_pot, gradient_pot = potentials(point_density, squared, core_density)
    scalar_part = 0.5 * weights * density_pot
    vector_part = 2.0 * weights * gradient_pot * gradient
    parts = jnp.concatenate([scalar_part[None], vector_part], axis=0)
    half = call(
        half_kernel, shape((row_count, points), BF16), [WHOLE] * 2,
        8 * basis_values.size, 4 * basis_values.size,
    )(masked, parts)

    product = 2 * row_count * points * share * count
    kept = count // 2
    block = (count, share, row_count)
    mirrored_found, earlier = {}, half
    for k in (2, 1):
        earlier = call(
            functools.partial(mirrored_other_kernel, share, count, k - 1), shape(block),
            [WHOLE, ANYWHERE, WHOLE], product, 3 * half.size,
        )(half, earlier, behind)
        mirrored_found[k] = swap(earlier, "col", 1)
    central_other = call(
        functools.partial(central_other_kernel, share, count), shape(block),
        [WHOLE] * 2 + [ANYWHERE], 2 * product, 4 * half.size,
    )(half, own, earlier)
    central_found = swap(central_other, "col", 1)
    mirrored_keep, mirrored_send = {}, {}
    for k in (2, 1):
        mirrored_keep[k], mirrored_send[k] = call(
            functools.partial(mirrored_own_kernel, share, count, k - 1),
            [shape((kept, share, row_count)), shape((kept, share, row_count), BF16)],
            [WHOLE] * 3, product, 4 * half.size,
        )(half, mirrored_found[k], behind)
    direct_other = call(
        functools.partial(direct_other_kernel, share, count), shape((REACH, *block)),
        [WHOLE, ANYWHERE, WHOLE], product * 2, 4 * half.size,
    )(half, central_other, ahead)
    direct_found = swap(direct_other, "col", 1)
    spare = max(share, 128)
    central_keep, central_send = call(
        functools.partial(central_own_kernel, share, count),
        [
            shape((kept, share, row_count)),
            shape((kept, share, row_count + spare), BF16),
        ],
        [WHOLE] * 3, product * 2, 4 * half.size,
    )(half, own, central_found)
    central_found = swap(central_send, "col", 2)
    direct_keep, direct_send = call(
        functools.partial(direct_own_kernel, share, count),
        [
            shape((REACH, kept, share, row_count)),
            shape((REACH, kept, share, row_count), BF16),
        ],
        [WHOLE] * 2 + [ANYWHERE, WHOLE], product * 2, 4 * half.size,
    )(half, direct_found, central_keep, ahead)

    def scatter(total, axis):
        bit = 4
        while bit < cols:
            paired = total.reshape(*total.shape[:axis], -1, 2, *total.shape[axis + 1 :])
            mine = (col // bit) % 2
            keep = lax.dynamic_index_in_dim(paired, mine, axis + 1, keepdims=False)
            send = lax.dynamic_index_in_dim(paired, 1 - mine, axis + 1, keepdims=False)
            total = keep + swap(send, "col", bit)
            bit *= 2
        return total

    mirrored = []
    for k in (2, 1):
        found = swap(mirrored_send[k], "col", 2)
        total = scatter(mirrored_keep[k] + found.astype(F32), 0).astype(BF16)
        mirrored.insert(0, from_ahead(total[0], k))
    found = swap(direct_send, "col", 2)
    partial = (central_keep, central_found, direct_keep, found)
    if kept > 1:
        total = call(
            functools.partial(joined_kernel, share), shape((kept, share, 3 * row_count)),
            [WHOLE] * 4, direct_keep.size, 8 * direct_keep.size,
        )(*partial)
        total = scatter(total, 0)[0]
        zero = jnp.zeros((share, row_count), BF16)
        return total + jnp.concatenate([zero, *mirrored], axis=1).astype(F32)
    return call(
        functools.partial(final_kernel, share), shape((1, share, 3 * row_count)),
        [WHOLE] * (4 + REACH), direct_keep.size, 10 * direct_keep.size,
    )(*partial, *mirrored)[0]


def solution(mesh):
    in_specs = (
        P(None, "row", "col"),
        P("row", None),
        P("row", "col"),
        P("col"),
        P(),
        P("col"),
        P("col"),
    )
    out_specs = P(("row", "col"), None)

    return jax.shard_map(body, mesh=mesh, in_specs=in_specs, out_specs=out_specs, check_vma=False)
```

```python
import functools
import math

import jax
import jax.numpy as jnp
from jax import lax
from jax.experimental import pallas as pl
from jax.experimental.pallas import tpu as pltpu
from jax.sharding import PartitionSpec as P


BAND = 5
REACH = BAND // 2

KAPPA_VALUE = 0.804
MU_VALUE = 0.22
SLATER_COEF = 0.7386


WHOLE = pl.BlockSpec(memory_space=pltpu.VMEM)
SCALARS = pl.BlockSpec(memory_space=pltpu.SMEM)
ANYWHERE = pl.BlockSpec(memory_space=pl.ANY)
PARAMS = pltpu.CompilerParams(vmem_limit_bytes=20 << 20)
F32 = jnp.float32
BF16 = jnp.bfloat16


def from_ahead(block, distance):
    size = lax.axis_size("row")
    return lax.ppermute(block, "row", [((i + distance) % size, i) for i in range(size)])


def from_side(block, distance):
    size = lax.axis_size("row")
    route = [((i + (distance if i % 2 == 0 else -distance)) % size, i) for i in range(size)]
    return lax.ppermute(block, "row", route)


def swap(block, axis, bit):
    return lax.ppermute(block, axis, [(i, i ^ bit) for i in range(lax.axis_size(axis))])


def energy_density(density_in, squared_in, core):
    regular = jnp.sqrt(density_in * density_in + core * core)
    reduced = squared_in * regular ** (-8.0 / 3.0)
    enhance = 1.0 + KAPPA_VALUE - KAPPA_VALUE / (1.0 + MU_VALUE * reduced / KAPPA_VALUE)
    return -SLATER_COEF * regular ** (4.0 / 3.0) * enhance


def potentials(density_in, squared_in, core):

    def total_energy(first_arg, second_arg):
        return jnp.sum(energy_density(first_arg, second_arg, core))

    return jax.grad(total_energy, argnums=(0, 1))(density_in, squared_in)


def call(kernel, outs, in_specs, flops, bytes_accessed, out_specs=None, scratch=()):
    return pl.pallas_call(
        kernel,
        out_shape=outs,
        in_specs=in_specs,
        out_specs=jax.tree.map(lambda _: WHOLE, outs) if out_specs is None else out_specs,
        scratch_shapes=list(scratch),
        compiler_params=PARAMS,
        cost_estimate=pl.CostEstimate(
            flops=int(flops), bytes_accessed=int(bytes_accessed), transcendentals=0
        ),
    )


def dot(left, right):
    return jnp.dot(left, right, preferred_element_type=F32)


def dot_rows(left, right):
    return lax.dot_general(left, right, (((1,), (1,)), ((), ())), preferred_element_type=F32)


def position():
    col = lax.axis_index("col")
    return lax.axis_index("row") % 2, col % 2, (col // 2) % 2


def mask_kernel(sb, gb, screen_hbm, basis_ref, own_ref, *rest):
    chunk_refs, (screen_ref, tile_ref, sem, sems) = rest[:-4], rest[-4:]
    row_count, _ = own_ref.shape
    screen_copy = pltpu.make_async_copy(screen_hbm, screen_ref, sem)
    screen_copy.start()
    copies = []
    for row in range(row_count // sb):
        window = pl.ds(row * sb, sb)
        copy = pltpu.make_async_copy(basis_ref.at[0, window], tile_ref.at[window], sems.at[row])
        copy.start()
        copies.append(copy)
    screen_copy.wait()
    for row, copy in enumerate(copies):
        rows = slice(row * sb, (row + 1) * sb)
        copy.wait()
        col = 0
        for chunk in chunk_refs:
            for start in range(0, chunk.shape[1], gb):
                keep = screen_ref[row, col // gb].astype(F32)
                tile = (tile_ref[rows, col : col + gb].astype(F32) * keep).astype(BF16)
                own_ref[rows, col : col + gb] = tile
                chunk[rows, start : start + gb] = tile
                col += gb


def split_kernel(density_ref, high_ref, low_ref):
    size = density_ref.shape[0]
    for column in range(BAND):
        strip = density_ref[:, column * size : (column + 1) * size]
        high = strip.astype(BF16)
        high_ref[column] = high
        low_ref[column] = (strip - high.astype(F32)).astype(BF16)


def both(high_ref, low_ref, column, block):
    return dot(high_ref[column], block) + dot(low_ref[column], block)


def early_kernel(start, high_ref, low_ref, own, beside, near, total_ref):
    sign = 1 - 2 * position()[0]
    cols = slice(start, start + near.shape[1])
    total_ref[...] = (
        both(high_ref, low_ref, REACH, own[:, cols])
        + both(high_ref, low_ref, REACH + sign, beside[:, cols])
        + both(high_ref, low_ref, REACH + 2 * sign, near[...])
    )


def later_kernel(high_ref, low_ref, partial_ref, across, total_ref):
    sign = 1 - 2 * position()[0]
    total_ref[...] = partial_ref[...] + both(high_ref, low_ref, REACH - sign, across[...])


def sums_kernel(start, high_ref, low_ref, partial_ref, far, masked_ref, sums_ref, total_ref):
    sign = 1 - 2 * position()[0]
    width = far.shape[1]
    total_ref[...] = partial_ref[...] + both(high_ref, low_ref, REACH - 2 * sign, far[...])
    for c in range(masked_ref.shape[0]):
        product = masked_ref[c, :, start : start + width] * total_ref[...]
        sums_ref[c : c + 1, :] = jnp.sum(product, axis=0, keepdims=True)


def widen_kernel(sb, gb, screen_ref, basis_ref, masked_ref):
    components, row_count, points = basis_ref.shape
    for part in range(points // gb):
        cols = slice(part * gb, (part + 1) * gb)
        for row in range(row_count // sb):
            rows = slice(row * sb, (row + 1) * sb)
            keep = screen_ref[row, part].astype(F32)
            for c in range(components):
                masked_ref[c, rows, cols] = basis_ref[c, rows, cols].astype(F32) * keep


def half_kernel(masked_ref, parts_ref, half_ref):
    components, row_count, points = masked_ref.shape
    for start in range(0, points, 128):
        cols = slice(start, start + 128)
        for row in range(0, row_count, 128):
            rows = slice(row, row + 128)
            total = parts_ref[0:1, cols] * masked_ref[0, rows, cols]
            for c in range(1, components):
                total += parts_ref[c : c + 1, cols] * masked_ref[c, rows, cols]
            half_ref[rows, cols] = total.astype(BF16)


def sorted_kernel(chunks, beside, *refs):
    near, far, across = (refs[i * chunks : (i + 1) * chunks] for i in range(3))
    ahead_ref, behind_ref = refs[3 * chunks :]

    def fill(here_ref, there_ref):
        here_ref[0] = beside[...]
        start = 0
        for one, two, three in zip(near, across, far):
            cols = slice(start, start + one.shape[1])
            here_ref[1, :, cols] = one[...]
            there_ref[0, :, cols] = two[...]
            there_ref[1, :, cols] = three[...]
            start += one.shape[1]

    odd = position()[0]

    @pl.when(odd == 0)
    def _():
        fill(ahead_ref, behind_ref)

    @pl.when(odd != 0)
    def _():
        fill(behind_ref, ahead_ref)


def rows_of(ref, side, share, count):
    blocks = []
    for step in range(count):
        window = pl.ds(pl.multiple_of((2 * step + side) * share, share), share)
        blocks.append(ref[window, :])
    return jnp.concatenate(blocks, axis=0) if count > 1 else blocks[0]


def mirrored_product(half_ref, block, side, share, count):
    total = dot_rows(rows_of(block, side, share, count), half_ref[...])
    return total.reshape(count, share, half_ref.shape[0])


def central_product(half_ref, own, side, share, count):
    total = dot_rows(rows_of(own, side, share, count), half_ref[...])
    total += dot_rows(rows_of(half_ref, side, share, count), own[...])
    return total.reshape(count, share, half_ref.shape[0])


def direct_product(half_ref, block, side, share, count):
    total = dot_rows(rows_of(half_ref, side, share, count), block[...])
    return total.reshape(count, share, half_ref.shape[0])


def deposit(total, side, keep_ref, send_ref):
    for step in range(total.shape[-3] // 2):
        low, high = total[..., 2 * step, :, :], total[..., 2 * step + 1, :, :]
        keep_ref[..., step, :, :] = jnp.where(side == 0, low, high)
        send_ref[..., step, :, :] = jnp.where(side == 0, high, low).astype(send_ref.dtype)


def mirrored_other_kernel(share, count, k, half_ref, earlier_ref, behind_ref, out):
    side = 1 - position()[1]
    out[...] = mirrored_product(half_ref, behind_ref.at[k], side, share, count)


def mirrored_own_kernel(share, count, k, half_ref, found_ref, behind_ref, keep_ref, send_ref):
    _, core, side = position()
    total = mirrored_product(half_ref, behind_ref.at[k], core, share, count)
    deposit(total + found_ref[...], side, keep_ref, send_ref)


def central_other_kernel(share, count, half_ref, own, earlier_ref, out):
    out[...] = central_product(half_ref, own, 1 - position()[1], share, count)


def direct_other_kernel(share, count, half_ref, earlier_ref, ahead_ref, out):
    side = 1 - position()[1]
    for k in range(REACH):
        out[k] = direct_product(half_ref, ahead_ref.at[k], side, share, count)


def diagonal_tiles(quarter, share, size, run):
    width = max(share, 128)
    for block in range(size // width):

        @pl.when((quarter * share) // width == block)
        def _():
            row = lax.broadcasted_iota(jnp.int32, (share, width), 0)
            lane = lax.broadcasted_iota(jnp.int32, (share, width), 1)
            run(slice(block * width, (block + 1) * width), lane == row + quarter * share - block * width)


def central_own_kernel(share, count, half_ref, own, found_ref, keep_ref, send_ref):
    _, core, side = position()
    size = half_ref.shape[0]
    total = central_product(half_ref, own, core, share, count) + found_ref[...]
    for step in range(count // 2):
        low, high = total[2 * step], total[2 * step + 1]
        keep_ref[step] = jnp.where(side == 0, low, high)
        send = jnp.where(side == 0, high, low)
        rounded = send.astype(BF16)
        send_ref[step, :share, :] = rounded
        send_ref[step, share:, :] = jnp.zeros((send_ref.shape[1] - share, size), BF16)

        def store(cols, mask):
            rest = jnp.where(mask, send[:, cols] - rounded[:, cols].astype(F32), 0.0)
            rest = jnp.sum(rest, axis=0, keepdims=True)
            rest = jnp.broadcast_to(rest, (send_ref.shape[1] - share, rest.shape[1]))
            send_ref[step, share:, : rest.shape[1]] = rest.astype(BF16)

        diagonal_tiles((2 * step + 1 - side) * 2 + core, share, size, store)


def direct_own_kernel(share, count, half_ref, found_ref, earlier_ref, ahead_ref, keep_ref, send_ref):
    _, core, side = position()
    for k in range(REACH):
        total = direct_product(half_ref, ahead_ref.at[k], core, share, count) + found_ref[k]
        deposit(total, side, keep_ref.at[k], send_ref.at[k])


def central_sum(share, step, central_ref, found_ref, out_ref):
    _, core, side = position()
    size = central_ref.shape[-1]
    out_ref[step, :, :size] = central_ref[step] + found_ref[step, :share, :].astype(F32)

    def add(cols, mask):
        width = mask.shape[1]
        rest = found_ref[step, share : share + 16, :width].astype(F32)[0:1]
        out_ref[step, :, cols] += jnp.where(mask, jnp.broadcast_to(rest, mask.shape), 0.0)

    diagonal_tiles((2 * step + side) * 2 + core, share, size, add)


def joined_kernel(share, central_ref, found_ref, keep_ref, direct_ref, out_ref):
    size = keep_ref.shape[-1]
    for step in range(found_ref.shape[0]):
        central_sum(share, step, central_ref, found_ref, out_ref)
        for k in range(REACH):
            cols = slice((k + 1) * size, (k + 2) * size)
            out_ref[step, :, cols] = keep_ref[k, step] + direct_ref[k, step].astype(F32)


def final_kernel(share, central_ref, found_ref, keep_ref, direct_ref, one, two, out_hbm, out_ref, sems):
    size = keep_ref.shape[-1]
    copies = []

    def release(k):
        cols = slice(k * size, (k + 1) * size)
        copy = pltpu.make_async_copy(out_ref.at[:, :, cols], out_hbm.at[:, :, cols], sems.at[k])
        copy.start()
        copies.append(copy)

    for k, block in enumerate((one, two)):
        cols = slice((k + 1) * size, (k + 2) * size)
        out_ref[0, :, cols] = (
            keep_ref[k, 0] + direct_ref[k, 0].astype(F32) + block[...].astype(F32)
        )
        release(k + 1)
    central_sum(share, 0, central_ref, found_ref, out_ref)
    release(0)
    for copy in copies:
        copy.wait()


def shape(dims, kind=F32):
    return jax.ShapeDtypeStruct(dims, kind)


def body(basis_values, density, screen, atom_of_block, atom_factor, quad_weight, core_density):
    rows, cols = lax.axis_size("row"), lax.axis_size("col")
    col = lax.axis_index("col")
    components, row_count, points = basis_values.shape
    sb, gb = row_count // screen.shape[0], points // screen.shape[1]
    eighth = max(1, screen.shape[1] // 8) * gb
    widths = (points - 3 * eighth, 2 * eighth, eighth)
    chunks = len(widths)
    share, count = row_count // cols, cols // 2
    square = 2 * row_count * row_count

    own, *mine = call(
        functools.partial(mask_kernel, sb, gb),
        [shape((row_count, width), BF16) for width in (points, *widths)],
        [pl.BlockSpec(memory_space=pltpu.HBM)] * 2, row_count * points, 6 * row_count * points,
        scratch=[
            pltpu.SMEM(screen.shape, jnp.int32),
            pltpu.VMEM((row_count, points), BF16),
            pltpu.SemaphoreType.DMA,
            pltpu.SemaphoreType.DMA((screen.shape[0],)),
        ],
    )(pltpu.with_memory_space_constraint(screen, pltpu.HBM), pltpu.with_memory_space_constraint(basis_values, pltpu.HBM))
    near, far, across = [], [], []
    for chunk, block in enumerate(mine):
        near.append(from_side(block, 2))
        far.append(from_side(block, -2))
        across.append(swap(near[chunk], "row", 1))
    beside = swap(own, "row", 1)

    high, low = call(
        split_kernel, [shape((BAND, row_count, row_count), BF16)] * 2, [WHOLE],
        density.size * 4, density.size * 8,
    )(density)
    masked = call(
        functools.partial(widen_kernel, sb, gb), shape(basis_values.shape), [SCALARS, WHOLE],
        basis_values.size, 6 * basis_values.size,
    )(screen, basis_values)
    sums, first = [], 0
    for chunk, width in enumerate(widths):
        total = shape((row_count, width))
        partial = call(
            functools.partial(early_kernel, first), total, [WHOLE] * 5,
            6 * square * width, 10 * square,
        )(high, low, own, beside, near[chunk])
        partial = call(later_kernel, total, [WHOLE] * 4, 2 * square * width, 4 * square)(
            high, low, partial, across[chunk]
        )
        found = call(
            functools.partial(sums_kernel, first), shape((components, width)),
            [WHOLE] * 5, 2 * square * width, 6 * square,
            scratch=[pltpu.VMEM((row_count, width), F32)],
        )(high, low, partial, far[chunk], masked)
        sums.append(found)
        first += width
    ahead, behind = call(
        functools.partial(sorted_kernel, chunks),
        [shape((REACH, row_count, points), BF16)] * 2, [WHOLE] * (1 + 3 * chunks),
        row_count * points, 16 * row_count * points,
    )(beside, *near, *far, *across)
    summed = jnp.concatenate(sums, axis=1)
    groups = [(1, 2, 3)] + [(1 << bit,) for bit in range(2, rows.bit_length() - 1)]
    for group in groups:
        found = []
        for distance in group:
            found.append(swap(summed, "row", distance))
        for other in found:
            summed = summed + other

    point_density = summed[0]
    gradient = 2.0 * summed[1:]
    squared = jnp.sum(gradient * gradient, axis=0)
    atoms = atom_factor.shape[0]
    chooser = (atom_of_block[:, None] == jnp.arange(atoms, dtype=jnp.int32)[None, :]).astype(F32)
    block_factor = jnp.dot(chooser, atom_factor, precision=lax.Precision.HIGHEST)
    group_size = points // atom_of_block.shape[0]
    weights = (quad_weight.reshape(-1, group_size) * block_factor[:, None]).reshape(
        points
    ) / math.sqrt(points * cols)
    density_pot, gradient_pot = potentials(point_density, squared, core_density)
    scalar_part = 0.5 * weights * density_pot
    vector_part = 2.0 * weights * gradient_pot * gradient
    parts = jnp.concatenate([scalar_part[None], vector_part], axis=0)
    half = call(
        half_kernel, shape((row_count, points), BF16), [WHOLE] * 2,
        8 * basis_values.size, 4 * basis_values.size,
    )(masked, parts)

    product = 2 * row_count * points * share * count
    kept = count // 2
    block = (count, share, row_count)
    mirrored_found, earlier = {}, half
    for k in (2, 1):
        earlier = call(
            functools.partial(mirrored_other_kernel, share, count, k - 1), shape(block),
            [WHOLE, ANYWHERE, WHOLE], product, 3 * half.size,
        )(half, earlier, behind)
        mirrored_found[k] = swap(earlier, "col", 1)
    central_other = call(
        functools.partial(central_other_kernel, share, count), shape(block),
        [WHOLE] * 2 + [ANYWHERE], 2 * product, 4 * half.size,
    )(half, own, earlier)
    central_found = swap(central_other, "col", 1)
    mirrored_keep, mirrored_send = {}, {}
    for k in (2, 1):
        mirrored_keep[k], mirrored_send[k] = call(
            functools.partial(mirrored_own_kernel, share, count, k - 1),
            [shape((kept, share, row_count)), shape((kept, share, row_count), BF16)],
            [WHOLE] * 3, product, 4 * half.size,
        )(half, mirrored_found[k], behind)
    direct_other = call(
        functools.partial(direct_other_kernel, share, count), shape((REACH, *block)),
        [WHOLE, ANYWHERE, WHOLE], product * 2, 4 * half.size,
    )(half, central_other, ahead)
    direct_found = swap(direct_other, "col", 1)
    central_keep, central_send = call(
        functools.partial(central_own_kernel, share, count),
        [
            shape((kept, share, row_count)),
            shape((kept, share + 16, row_count), BF16),
        ],
        [WHOLE] * 3, product * 2, 4 * half.size,
    )(half, own, central_found)
    central_found = swap(central_send, "col", 2)
    direct_keep, direct_send = call(
        functools.partial(direct_own_kernel, share, count),
        [
            shape((REACH, kept, share, row_count)),
            shape((REACH, kept, share, row_count), BF16),
        ],
        [WHOLE] * 2 + [ANYWHERE, WHOLE], product * 2, 4 * half.size,
    )(half, direct_found, central_keep, ahead)

    def scatter(total, axis):
        bit = 4
        while bit < cols:
            paired = total.reshape(*total.shape[:axis], -1, 2, *total.shape[axis + 1 :])
            mine = (col // bit) % 2
            keep = lax.dynamic_index_in_dim(paired, mine, axis + 1, keepdims=False)
            send = lax.dynamic_index_in_dim(paired, 1 - mine, axis + 1, keepdims=False)
            total = keep + swap(send, "col", bit)
            bit *= 2
        return total

    mirrored = []
    for k in (2, 1):
        found = swap(mirrored_send[k], "col", 2)
        total = scatter(mirrored_keep[k] + found.astype(F32), 0).astype(BF16)
        mirrored.insert(0, from_ahead(total[0], k))
    found = swap(direct_send, "col", 2)
    partial = (central_keep, central_found, direct_keep, found)
    if kept > 1:
        total = call(
            functools.partial(joined_kernel, share), shape((kept, share, 3 * row_count)),
            [WHOLE] * 4, direct_keep.size, 8 * direct_keep.size,
        )(*partial)
        total = scatter(total, 0)[0]
        zero = jnp.zeros((share, row_count), BF16)
        return total + jnp.concatenate([zero, *mirrored], axis=1).astype(F32)
    return call(
        functools.partial(final_kernel, share), shape((1, share, 3 * row_count)),
        [WHOLE] * (4 + REACH), direct_keep.size, 10 * direct_keep.size, out_specs=ANYWHERE,
        scratch=[
            pltpu.VMEM((1, share, 3 * row_count), F32),
            pltpu.SemaphoreType.DMA((3,)),
        ],
    )(*partial, *mirrored)[0]


def solution(mesh):
    in_specs = (
        P(None, "row", "col"),
        P("row", None),
        P("row", "col"),
        P("col"),
        P(),
        P("col"),
        P("col"),
    )
    out_specs = P(("row", "col"), None)

    return jax.shard_map(body, mesh=mesh, in_specs=in_specs, out_specs=out_specs, check_vma=False)
```

```python
import functools
import math

import jax
import jax.numpy as jnp
from jax import lax
from jax.experimental import pallas as pl
from jax.experimental.pallas import tpu as pltpu
from jax.sharding import PartitionSpec as P


BAND = 5
REACH = BAND // 2

KAPPA_VALUE = 0.804
MU_VALUE = 0.22
SLATER_COEF = 0.7386


WHOLE = pl.BlockSpec(memory_space=pltpu.VMEM)
SCALARS = pl.BlockSpec(memory_space=pltpu.SMEM)
ANYWHERE = pl.BlockSpec(memory_space=pl.ANY)
PARAMS = pltpu.CompilerParams(vmem_limit_bytes=20 << 20)
F32 = jnp.float32
BF16 = jnp.bfloat16


def from_ahead(block, distance):
    size = lax.axis_size("row")
    return lax.ppermute(block, "row", [((i + distance) % size, i) for i in range(size)])


def from_side(block, distance):
    size = lax.axis_size("row")
    route = [((i + (distance if i % 2 == 0 else -distance)) % size, i) for i in range(size)]
    return lax.ppermute(block, "row", route)


def swap(block, axis, bit):
    return lax.ppermute(block, axis, [(i, i ^ bit) for i in range(lax.axis_size(axis))])


def energy_density(density_in, squared_in, core):
    regular = jnp.sqrt(density_in * density_in + core * core)
    reduced = squared_in * regular ** (-8.0 / 3.0)
    enhance = 1.0 + KAPPA_VALUE - KAPPA_VALUE / (1.0 + MU_VALUE * reduced / KAPPA_VALUE)
    return -SLATER_COEF * regular ** (4.0 / 3.0) * enhance


def potentials(density_in, squared_in, core):

    def total_energy(first_arg, second_arg):
        return jnp.sum(energy_density(first_arg, second_arg, core))

    return jax.grad(total_energy, argnums=(0, 1))(density_in, squared_in)


def call(kernel, outs, in_specs, flops, bytes_accessed, out_specs=None, scratch=()):
    return pl.pallas_call(
        kernel,
        out_shape=outs,
        in_specs=in_specs,
        out_specs=jax.tree.map(lambda _: WHOLE, outs) if out_specs is None else out_specs,
        scratch_shapes=list(scratch),
        compiler_params=PARAMS,
        cost_estimate=pl.CostEstimate(
            flops=int(flops), bytes_accessed=int(bytes_accessed), transcendentals=0
        ),
    )


def dot(left, right):
    return jnp.dot(left, right, preferred_element_type=F32)


def dot_rows(left, right):
    return lax.dot_general(left, right, (((1,), (1,)), ((), ())), preferred_element_type=F32)


def position():
    col = lax.axis_index("col")
    return lax.axis_index("row") % 2, col % 2, (col // 2) % 2


def mask_kernel(sb, gb, screen_hbm, basis_ref, own_ref, *rest):
    chunk_refs, (screen_ref, tile_ref, sem, sems) = rest[:-4], rest[-4:]
    row_count, _ = own_ref.shape
    screen_copy = pltpu.make_async_copy(screen_hbm, screen_ref, sem)
    screen_copy.start()
    copies = []
    for row in range(row_count // sb):
        window = pl.ds(row * sb, sb)
        copy = pltpu.make_async_copy(basis_ref.at[0, window], tile_ref.at[window], sems.at[row])
        copy.start()
        copies.append(copy)
    screen_copy.wait()
    for row, copy in enumerate(copies):
        rows = slice(row * sb, (row + 1) * sb)
        copy.wait()
        col = 0
        for chunk in chunk_refs:
            for start in range(0, chunk.shape[1], gb):
                keep = screen_ref[row, col // gb].astype(F32)
                tile = tile_ref[rows, col : col + gb] * jnp.full((sb, gb), keep).astype(BF16)
                own_ref[rows, col : col + gb] = tile
                chunk[rows, start : start + gb] = tile
                col += gb


def split_kernel(density_ref, high_ref, low_ref):
    size = density_ref.shape[0]
    for column in range(BAND):
        strip = density_ref[:, column * size : (column + 1) * size]
        high = strip.astype(BF16)
        high_ref[column] = high
        low_ref[column] = (strip - high.astype(F32)).astype(BF16)


def both(high_ref, low_ref, column, block):
    return dot(high_ref[column], block) + dot(low_ref[column], block)


def early_kernel(start, high_ref, low_ref, own, beside, near, total_ref):
    sign = 1 - 2 * position()[0]
    cols = slice(start, start + near.shape[1])
    total_ref[...] = (
        both(high_ref, low_ref, REACH, own[:, cols])
        + both(high_ref, low_ref, REACH + sign, beside[:, cols])
        + both(high_ref, low_ref, REACH + 2 * sign, near[...])
    )


def later_kernel(high_ref, low_ref, partial_ref, across, total_ref):
    sign = 1 - 2 * position()[0]
    total_ref[...] = partial_ref[...] + both(high_ref, low_ref, REACH - sign, across[...])


def sums_kernel(start, high_ref, low_ref, partial_ref, far, masked_ref, sums_ref, total_ref):
    sign = 1 - 2 * position()[0]
    width = far.shape[1]
    total_ref[...] = partial_ref[...] + both(high_ref, low_ref, REACH - 2 * sign, far[...])
    for c in range(masked_ref.shape[0]):
        product = masked_ref[c, :, start : start + width] * total_ref[...]
        sums_ref[c : c + 1, :] = jnp.sum(product, axis=0, keepdims=True)


def widen_kernel(sb, gb, screen_ref, basis_ref, masked_ref):
    components, row_count, points = basis_ref.shape
    for part in range(points // gb):
        cols = slice(part * gb, (part + 1) * gb)
        for row in range(row_count // sb):
            rows = slice(row * sb, (row + 1) * sb)
            keep = screen_ref[row, part].astype(F32)
            for c in range(components):
                masked_ref[c, rows, cols] = basis_ref[c, rows, cols].astype(F32) * keep


def half_kernel(share, count, step, masked_ref, parts_ref, behind_ref, half_ref, *outs):
    components, row_count, points = masked_ref.shape
    side = 1 - position()[1]
    for first in range(0, points, step):
        for start in range(first, first + step, 128):
            cols = slice(start, start + 128)
            for row in range(0, row_count, 128):
                rows = slice(row, row + 128)
                total = parts_ref[0:1, cols] * masked_ref[0, rows, cols]
                for c in range(1, components):
                    total += parts_ref[c : c + 1, cols] * masked_ref[c, rows, cols]
                half_ref[rows, cols] = total.astype(BF16)
        cols = slice(first, first + step)
        for k, out in outs_of(outs):
            left = jnp.concatenate(
                [
                    behind_ref[k, pl.ds(pl.multiple_of((2 * i + side) * share, share), share), cols]
                    for i in range(count)
                ],
                axis=0,
            )
            found = dot_rows(left, half_ref[:, cols]).reshape(out.shape)
            out[...] = found if first == 0 else out[...] + found


def outs_of(outs):
    return tuple(zip((1, 0), outs))


def sorted_kernel(chunks, beside, *refs):
    near, far, across = (refs[i * chunks : (i + 1) * chunks] for i in range(3))
    ahead_ref, behind_ref = refs[3 * chunks :]

    def fill(here_ref, there_ref):
        here_ref[0] = beside[...]
        start = 0
        for one, two, three in zip(near, across, far):
            cols = slice(start, start + one.shape[1])
            here_ref[1, :, cols] = one[...]
            there_ref[0, :, cols] = two[...]
            there_ref[1, :, cols] = three[...]
            start += one.shape[1]

    odd = position()[0]

    @pl.when(odd == 0)
    def _():
        fill(ahead_ref, behind_ref)

    @pl.when(odd != 0)
    def _():
        fill(behind_ref, ahead_ref)


def rows_of(ref, side, share, count):
    blocks = []
    for step in range(count):
        window = pl.ds(pl.multiple_of((2 * step + side) * share, share), share)
        blocks.append(ref[window, :])
    return jnp.concatenate(blocks, axis=0) if count > 1 else blocks[0]


def mirrored_product(half_ref, block, side, share, count):
    total = dot_rows(rows_of(block, side, share, count), half_ref[...])
    return total.reshape(count, share, half_ref.shape[0])


def central_product(half_ref, own, side, share, count):
    total = dot_rows(rows_of(own, side, share, count), half_ref[...])
    total += dot_rows(rows_of(half_ref, side, share, count), own[...])
    return total.reshape(count, share, half_ref.shape[0])


def direct_product(half_ref, block, side, share, count):
    total = dot_rows(rows_of(half_ref, side, share, count), block[...])
    return total.reshape(count, share, half_ref.shape[0])


def deposit(total, side, keep_ref, send_ref):
    for step in range(total.shape[-3] // 2):
        low, high = total[..., 2 * step, :, :], total[..., 2 * step + 1, :, :]
        keep_ref[..., step, :, :] = jnp.where(side == 0, low, high)
        send_ref[..., step, :, :] = jnp.where(side == 0, high, low).astype(send_ref.dtype)


def mirrored_other_kernel(share, count, k, half_ref, earlier_ref, behind_ref, out):
    side = 1 - position()[1]
    out[...] = mirrored_product(half_ref, behind_ref.at[k], side, share, count)


def mirrored_own_kernel(share, count, k, half_ref, found_ref, behind_ref, keep_ref, send_ref):
    _, core, side = position()
    total = mirrored_product(half_ref, behind_ref.at[k], core, share, count)
    deposit(total + found_ref[...], side, keep_ref, send_ref)


def central_other_kernel(share, count, half_ref, own, earlier_ref, out):
    out[...] = central_product(half_ref, own, 1 - position()[1], share, count)


def direct_other_kernel(share, count, half_ref, earlier_ref, ahead_ref, out):
    side = 1 - position()[1]
    for k in range(REACH):
        out[k] = direct_product(half_ref, ahead_ref.at[k], side, share, count)


def diagonal_tiles(quarter, share, size, run):
    width = max(share, 128)
    for block in range(size // width):

        @pl.when((quarter * share) // width == block)
        def _():
            row = lax.broadcasted_iota(jnp.int32, (share, width), 0)
            lane = lax.broadcasted_iota(jnp.int32, (share, width), 1)
            run(slice(block * width, (block + 1) * width), lane == row + quarter * share - block * width)


def central_own_kernel(share, count, half_ref, own, found_ref, keep_ref, send_ref):
    _, core, side = position()
    size = half_ref.shape[0]
    total = central_product(half_ref, own, core, share, count) + found_ref[...]
    for step in range(count // 2):
        low, high = total[2 * step], total[2 * step + 1]
        keep_ref[step] = jnp.where(side == 0, low, high)
        send = jnp.where(side == 0, high, low)
        rounded = send.astype(BF16)
        send_ref[step, :share, :] = rounded
        send_ref[step, share:, :] = jnp.zeros((send_ref.shape[1] - share, size), BF16)

        def store(cols, mask):
            rest = jnp.where(mask, send[:, cols] - rounded[:, cols].astype(F32), 0.0)
            rest = jnp.sum(rest, axis=0, keepdims=True)
            rest = jnp.broadcast_to(rest, (send_ref.shape[1] - share, rest.shape[1]))
            send_ref[step, share:, : rest.shape[1]] = rest.astype(BF16)

        diagonal_tiles((2 * step + 1 - side) * 2 + core, share, size, store)


def direct_own_kernel(share, count, half_ref, found_ref, earlier_ref, ahead_ref, keep_ref, send_ref):
    _, core, side = position()
    for k in range(REACH):
        total = direct_product(half_ref, ahead_ref.at[k], core, share, count) + found_ref[k]
        deposit(total, side, keep_ref.at[k], send_ref.at[k])


def central_sum(share, step, central_ref, found_ref, out_ref):
    _, core, side = position()
    size = central_ref.shape[-1]
    out_ref[step, :, :size] = central_ref[step] + found_ref[step, :share, :].astype(F32)

    def add(cols, mask):
        width = mask.shape[1]
        rest = found_ref[step, share : share + 16, :width].astype(F32)[0:1]
        out_ref[step, :, cols] += jnp.where(mask, jnp.broadcast_to(rest, mask.shape), 0.0)

    diagonal_tiles((2 * step + side) * 2 + core, share, size, add)


def joined_kernel(share, central_ref, found_ref, keep_ref, direct_ref, out_ref):
    size = keep_ref.shape[-1]
    for step in range(found_ref.shape[0]):
        central_sum(share, step, central_ref, found_ref, out_ref)
        for k in range(REACH):
            cols = slice((k + 1) * size, (k + 2) * size)
            out_ref[step, :, cols] = keep_ref[k, step] + direct_ref[k, step].astype(F32)


def final_kernel(share, central_ref, found_ref, keep_ref, direct_ref, one, two, out_hbm, out_ref, sems):
    size = keep_ref.shape[-1]
    copies = []

    def release(k):
        cols = slice(k * size, (k + 1) * size)
        copy = pltpu.make_async_copy(out_ref.at[:, :, cols], out_hbm.at[:, :, cols], sems.at[k])
        copy.start()
        copies.append(copy)

    for k, block in enumerate((one, two)):
        cols = slice((k + 1) * size, (k + 2) * size)
        out_ref[0, :, cols] = (
            keep_ref[k, 0] + direct_ref[k, 0].astype(F32) + block[...].astype(F32)
        )
        release(k + 1)
    central_sum(share, 0, central_ref, found_ref, out_ref)
    release(0)
    for copy in copies:
        copy.wait()


def shape(dims, kind=F32):
    return jax.ShapeDtypeStruct(dims, kind)


def body(basis_values, density, screen, atom_of_block, atom_factor, quad_weight, core_density):
    rows, cols = lax.axis_size("row"), lax.axis_size("col")
    col = lax.axis_index("col")
    components, row_count, points = basis_values.shape
    sb, gb = row_count // screen.shape[0], points // screen.shape[1]
    eighth = max(1, screen.shape[1] // 8) * gb
    widths = (points - 3 * eighth, 2 * eighth, eighth)
    chunks = len(widths)
    share, count = row_count // cols, cols // 2
    square = 2 * row_count * row_count

    own, *mine = call(
        functools.partial(mask_kernel, sb, gb),
        [shape((row_count, width), BF16) for width in (points, *widths)],
        [pl.BlockSpec(memory_space=pltpu.HBM)] * 2, row_count * points, 6 * row_count * points,
        scratch=[
            pltpu.SMEM(screen.shape, jnp.int32),
            pltpu.VMEM((row_count, points), BF16),
            pltpu.SemaphoreType.DMA,
            pltpu.SemaphoreType.DMA((screen.shape[0],)),
        ],
    )(pltpu.with_memory_space_constraint(screen, pltpu.HBM), pltpu.with_memory_space_constraint(basis_values, pltpu.HBM))
    near, far, across = [], [], []
    for chunk, block in enumerate(mine):
        near.append(from_side(block, 2))
        far.append(from_side(block, -2))
        across.append(swap(near[chunk], "row", 1))
    beside = swap(own, "row", 1)

    high, low = call(
        split_kernel, [shape((BAND, row_count, row_count), BF16)] * 2, [WHOLE],
        density.size * 4, density.size * 8,
    )(density)
    masked = call(
        functools.partial(widen_kernel, sb, gb), shape(basis_values.shape), [SCALARS, WHOLE],
        basis_values.size, 6 * basis_values.size,
    )(screen, basis_values)
    sums, first = [], 0
    for chunk, width in enumerate(widths):
        total = shape((row_count, width))
        partial = call(
            functools.partial(early_kernel, first), total, [WHOLE] * 5,
            6 * square * width, 10 * square,
        )(high, low, own, beside, near[chunk])
        partial = call(later_kernel, total, [WHOLE] * 4, 2 * square * width, 4 * square)(
            high, low, partial, across[chunk]
        )
        found = call(
            functools.partial(sums_kernel, first), shape((components, width)),
            [WHOLE] * 5, 2 * square * width, 6 * square,
            scratch=[pltpu.VMEM((row_count, width), F32)],
        )(high, low, partial, far[chunk], masked)
        sums.append(found)
        first += width
    ahead, behind = call(
        functools.partial(sorted_kernel, chunks),
        [shape((REACH, row_count, points), BF16)] * 2, [WHOLE] * (1 + 3 * chunks),
        row_count * points, 16 * row_count * points,
    )(beside, *near, *far, *across)
    summed = jnp.concatenate(sums, axis=1)
    groups = [(1, 2, 3)] + [(1 << bit,) for bit in range(2, rows.bit_length() - 1)]
    for group in groups:
        found = []
        for distance in group:
            found.append(swap(summed, "row", distance))
        for other in found:
            summed = summed + other

    point_density = summed[0]
    gradient = 2.0 * summed[1:]
    squared = jnp.sum(gradient * gradient, axis=0)
    atoms = atom_factor.shape[0]
    chooser = (atom_of_block[:, None] == jnp.arange(atoms, dtype=jnp.int32)[None, :]).astype(F32)
    block_factor = jnp.dot(chooser, atom_factor, precision=lax.Precision.HIGHEST)
    group_size = points // atom_of_block.shape[0]
    weights = (quad_weight.reshape(-1, group_size) * block_factor[:, None]).reshape(
        points
    ) / math.sqrt(points * cols)
    density_pot, gradient_pot = potentials(point_density, squared, core_density)
    scalar_part = 0.5 * weights * density_pot
    vector_part = 2.0 * weights * gradient_pot * gradient
    parts = jnp.concatenate([scalar_part[None], vector_part], axis=0)
    product = 2 * row_count * points * share * count
    kept = count // 2
    block = (count, share, row_count)
    fused = 1
    half, *mirrored_other = call(
        functools.partial(half_kernel, share, count, 256),
        [shape((row_count, points), BF16)] + [shape(block)] * fused, [WHOLE] * 3,
        8 * basis_values.size + fused * product, 4 * basis_values.size,
    )(masked, parts, behind)
    mirrored_found, earlier = {}, half
    for k in (2, 1):
        if k > REACH - fused:
            earlier = mirrored_other[REACH - k]
        else:
            earlier = call(
                functools.partial(mirrored_other_kernel, share, count, k - 1), shape(block),
                [WHOLE, ANYWHERE, WHOLE], product, 3 * half.size,
            )(half, earlier, behind)
        mirrored_found[k] = swap(earlier, "col", 1)
    central_other = call(
        functools.partial(central_other_kernel, share, count), shape(block),
        [WHOLE] * 2 + [ANYWHERE], 2 * product, 4 * half.size,
    )(half, own, earlier)
    central_found = swap(central_other, "col", 1)
    mirrored_keep, mirrored_send = {}, {}
    for k in (2, 1):
        mirrored_keep[k], mirrored_send[k] = call(
            functools.partial(mirrored_own_kernel, share, count, k - 1),
            [shape((kept, share, row_count)), shape((kept, share, row_count), BF16)],
            [WHOLE] * 3, product, 4 * half.size,
        )(half, mirrored_found[k], behind)
    direct_other = call(
        functools.partial(direct_other_kernel, share, count), shape((REACH, *block)),
        [WHOLE, ANYWHERE, WHOLE], product * 2, 4 * half.size,
    )(half, central_other, ahead)
    direct_found = swap(direct_other, "col", 1)
    central_keep, central_send = call(
        functools.partial(central_own_kernel, share, count),
        [
            shape((kept, share, row_count)),
            shape((kept, share + 16, row_count), BF16),
        ],
        [WHOLE] * 3, product * 2, 4 * half.size,
    )(half, own, central_found)
    central_found = swap(central_send, "col", 2)
    direct_keep, direct_send = call(
        functools.partial(direct_own_kernel, share, count),
        [
            shape((REACH, kept, share, row_count)),
            shape((REACH, kept, share, row_count), BF16),
        ],
        [WHOLE] * 2 + [ANYWHERE, WHOLE], product * 2, 4 * half.size,
    )(half, direct_found, central_keep, ahead)

    def scatter(total, axis):
        bit = 4
        while bit < cols:
            paired = total.reshape(*total.shape[:axis], -1, 2, *total.shape[axis + 1 :])
            mine = (col // bit) % 2
            keep = lax.dynamic_index_in_dim(paired, mine, axis + 1, keepdims=False)
            send = lax.dynamic_index_in_dim(paired, 1 - mine, axis + 1, keepdims=False)
            total = keep + swap(send, "col", bit)
            bit *= 2
        return total

    mirrored = []
    for k in (2, 1):
        found = swap(mirrored_send[k], "col", 2)
        total = scatter(mirrored_keep[k] + found.astype(F32), 0).astype(BF16)
        mirrored.insert(0, from_ahead(total[0], k))
    found = swap(direct_send, "col", 2)
    partial = (central_keep, central_found, direct_keep, found)
    if kept > 1:
        total = call(
            functools.partial(joined_kernel, share), shape((kept, share, 3 * row_count)),
            [WHOLE] * 4, direct_keep.size, 8 * direct_keep.size,
        )(*partial)
        total = scatter(total, 0)[0]
        zero = jnp.zeros((share, row_count), BF16)
        return total + jnp.concatenate([zero, *mirrored], axis=1).astype(F32)
    return call(
        functools.partial(final_kernel, share), shape((1, share, 3 * row_count)),
        [WHOLE] * (4 + REACH), direct_keep.size, 10 * direct_keep.size, out_specs=ANYWHERE,
        scratch=[
            pltpu.VMEM((1, share, 3 * row_count), F32),
            pltpu.SemaphoreType.DMA((3,)),
        ],
    )(*partial, *mirrored)[0]


def solution(mesh):
    in_specs = (
        P(None, "row", "col"),
        P("row", None),
        P("row", "col"),
        P("col"),
        P(),
        P("col"),
        P("col"),
    )
    out_specs = P(("row", "col"), None)

    return jax.shard_map(body, mesh=mesh, in_specs=in_specs, out_specs=out_specs, check_vma=False)
```

```python
import functools
import math

import jax
import jax.numpy as jnp
from jax import lax
from jax.experimental import pallas as pl
from jax.experimental.pallas import tpu as pltpu
from jax.sharding import PartitionSpec as P


BAND = 5
REACH = BAND // 2

KAPPA_VALUE = 0.804
MU_VALUE = 0.22
SLATER_COEF = 0.7386


WHOLE = pl.BlockSpec(memory_space=pltpu.VMEM)
SCALARS = pl.BlockSpec(memory_space=pltpu.SMEM)
ANYWHERE = pl.BlockSpec(memory_space=pl.ANY)
PARAMS = pltpu.CompilerParams(vmem_limit_bytes=20 << 20)
F32 = jnp.float32
BF16 = jnp.bfloat16


def from_ahead(block, distance):
    size = lax.axis_size("row")
    return lax.ppermute(block, "row", [((i + distance) % size, i) for i in range(size)])


def from_side(block, distance):
    size = lax.axis_size("row")
    route = [((i + (distance if i % 2 == 0 else -distance)) % size, i) for i in range(size)]
    return lax.ppermute(block, "row", route)


def swap(block, axis, bit):
    return lax.ppermute(block, axis, [(i, i ^ bit) for i in range(lax.axis_size(axis))])


def energy_density(density_in, squared_in, core):
    regular = jnp.sqrt(density_in * density_in + core * core)
    reduced = squared_in * regular ** (-8.0 / 3.0)
    enhance = 1.0 + KAPPA_VALUE - KAPPA_VALUE / (1.0 + MU_VALUE * reduced / KAPPA_VALUE)
    return -SLATER_COEF * regular ** (4.0 / 3.0) * enhance


def potentials(density_in, squared_in, core):

    def total_energy(first_arg, second_arg):
        return jnp.sum(energy_density(first_arg, second_arg, core))

    return jax.grad(total_energy, argnums=(0, 1))(density_in, squared_in)


def call(kernel, outs, in_specs, flops, bytes_accessed, out_specs=None, scratch=()):
    return pl.pallas_call(
        kernel,
        out_shape=outs,
        in_specs=in_specs,
        out_specs=jax.tree.map(lambda _: WHOLE, outs) if out_specs is None else out_specs,
        scratch_shapes=list(scratch),
        compiler_params=PARAMS,
        cost_estimate=pl.CostEstimate(
            flops=int(flops), bytes_accessed=int(bytes_accessed), transcendentals=0
        ),
    )


def dot(left, right):
    return jnp.dot(left, right, preferred_element_type=F32)


def dot_rows(left, right):
    return lax.dot_general(left, right, (((1,), (1,)), ((), ())), preferred_element_type=F32)


def position():
    col = lax.axis_index("col")
    return lax.axis_index("row") % 2, col % 2, (col // 2) % 2


def mask_kernel(sb, gb, screen_hbm, basis_ref, own_ref, *rest):
    chunk_refs, (screen_ref, tile_ref, sem, sems) = rest[:-4], rest[-4:]
    row_count, _ = own_ref.shape
    screen_copy = pltpu.make_async_copy(screen_hbm, screen_ref, sem)
    screen_copy.start()
    copies = []
    for row in range(row_count // sb):
        window = pl.ds(row * sb, sb)
        copy = pltpu.make_async_copy(basis_ref.at[0, window], tile_ref.at[window], sems.at[row])
        copy.start()
        copies.append(copy)
    screen_copy.wait()
    for row, copy in enumerate(copies):
        rows = slice(row * sb, (row + 1) * sb)
        copy.wait()
        col = 0
        for chunk in chunk_refs:
            for start in range(0, chunk.shape[1], gb):
                keep = screen_ref[row, col // gb].astype(F32)
                tile = tile_ref[rows, col : col + gb] * jnp.full((sb, gb), keep).astype(BF16)
                own_ref[rows, col : col + gb] = tile
                chunk[rows, start : start + gb] = tile
                col += gb


def split_kernel(density_ref, high_ref, low_ref):
    size = density_ref.shape[0]
    for column in range(BAND):
        strip = density_ref[:, column * size : (column + 1) * size]
        high = strip.astype(BF16)
        high_ref[column] = high
        low_ref[column] = (strip - high.astype(F32)).astype(BF16)


def both(high_ref, low_ref, column, block):
    return dot(high_ref[column], block) + dot(low_ref[column], block)


def early_kernel(start, high_ref, low_ref, own, beside, near, total_ref):
    sign = 1 - 2 * position()[0]
    cols = slice(start, start + near.shape[1])
    total_ref[...] = (
        both(high_ref, low_ref, REACH, own[:, cols])
        + both(high_ref, low_ref, REACH + sign, beside[:, cols])
        + both(high_ref, low_ref, REACH + 2 * sign, near[...])
    )


def later_kernel(high_ref, low_ref, partial_ref, across, total_ref):
    sign = 1 - 2 * position()[0]
    total_ref[...] = partial_ref[...] + both(high_ref, low_ref, REACH - sign, across[...])


def sums_kernel(start, high_ref, low_ref, partial_ref, far, masked_ref, sums_ref, total_ref):
    sign = 1 - 2 * position()[0]
    width = far.shape[1]
    total_ref[...] = partial_ref[...] + both(high_ref, low_ref, REACH - 2 * sign, far[...])
    for c in range(masked_ref.shape[0]):
        product = masked_ref[c, :, start : start + width] * total_ref[...]
        sums_ref[c : c + 1, :] = jnp.sum(product, axis=0, keepdims=True)


def widen_kernel(sb, gb, screen_ref, basis_ref, masked_ref):
    components, row_count, points = basis_ref.shape
    for part in range(points // gb):
        cols = slice(part * gb, (part + 1) * gb)
        for row in range(row_count // sb):
            rows = slice(row * sb, (row + 1) * sb)
            keep = screen_ref[row, part].astype(F32)
            for c in range(components):
                masked_ref[c, rows, cols] = basis_ref[c, rows, cols].astype(F32) * keep


def half_kernel(share, count, step, masked_ref, parts_ref, behind_ref, half_ref, *outs):
    components, row_count, points = masked_ref.shape
    side = 1 - position()[1]
    for first in range(0, points, step):
        for start in range(first, first + step, 128):
            cols = slice(start, start + 128)
            for row in range(0, row_count, 128):
                rows = slice(row, row + 128)
                total = parts_ref[0:1, cols] * masked_ref[0, rows, cols]
                for c in range(1, components):
                    total += parts_ref[c : c + 1, cols] * masked_ref[c, rows, cols]
                half_ref[rows, cols] = total.astype(BF16)
        cols = slice(first, first + step)
        for k, out in outs_of(outs):
            left = jnp.concatenate(
                [
                    behind_ref[k, pl.ds(pl.multiple_of((2 * i + side) * share, share), share), cols]
                    for i in range(count)
                ],
                axis=0,
            )
            found = dot_rows(left, half_ref[:, cols]).reshape(out.shape)
            out[...] = found if first == 0 else out[...] + found


def outs_of(outs):
    return tuple(zip((1, 0), outs))


def sorted_kernel(chunks, beside, *refs):
    near, far, across = (refs[i * chunks : (i + 1) * chunks] for i in range(3))
    ahead_ref, behind_ref = refs[3 * chunks :]

    def fill(here_ref, there_ref):
        here_ref[0] = beside[...]
        start = 0
        for one, two, three in zip(near, across, far):
            cols = slice(start, start + one.shape[1])
            here_ref[1, :, cols] = one[...]
            there_ref[0, :, cols] = two[...]
            there_ref[1, :, cols] = three[...]
            start += one.shape[1]

    odd = position()[0]

    @pl.when(odd == 0)
    def _():
        fill(ahead_ref, behind_ref)

    @pl.when(odd != 0)
    def _():
        fill(behind_ref, ahead_ref)


def rows_of(ref, side, share, count):
    blocks = []
    for step in range(count):
        window = pl.ds(pl.multiple_of((2 * step + side) * share, share), share)
        blocks.append(ref[window, :])
    return jnp.concatenate(blocks, axis=0) if count > 1 else blocks[0]


def mirrored_product(half_ref, block, side, share, count):
    total = dot_rows(rows_of(block, side, share, count), half_ref[...])
    return total.reshape(count, share, half_ref.shape[0])


def central_product(half_ref, own, side, share, count):
    total = dot_rows(rows_of(own, side, share, count), half_ref[...])
    total += dot_rows(rows_of(half_ref, side, share, count), own[...])
    return total.reshape(count, share, half_ref.shape[0])


def direct_product(half_ref, block, side, share, count):
    total = dot_rows(rows_of(half_ref, side, share, count), block[...])
    return total.reshape(count, share, half_ref.shape[0])


def deposit(total, side, keep_ref, send_ref):
    for step in range(total.shape[-3] // 2):
        low, high = total[..., 2 * step, :, :], total[..., 2 * step + 1, :, :]
        keep_ref[..., step, :, :] = jnp.where(side == 0, low, high)
        send_ref[..., step, :, :] = jnp.where(side == 0, high, low).astype(send_ref.dtype)


def mirrored_other_kernel(share, count, k, half_ref, earlier_ref, behind_ref, out):
    side = 1 - position()[1]
    out[...] = mirrored_product(half_ref, behind_ref.at[k], side, share, count)


def mirrored_own_kernel(share, count, k, half_ref, found_ref, behind_ref, keep_ref, send_ref):
    _, core, side = position()
    total = mirrored_product(half_ref, behind_ref.at[k], core, share, count)
    deposit(total + found_ref[...], side, keep_ref, send_ref)


def central_other_kernel(share, count, half_ref, own, earlier_ref, out):
    out[...] = central_product(half_ref, own, 1 - position()[1], share, count)


def direct_other_kernel(share, count, half_ref, earlier_ref, ahead_ref, out):
    side = 1 - position()[1]
    for k in range(REACH):
        out[k] = direct_product(half_ref, ahead_ref.at[k], side, share, count)


def diagonal_tiles(quarter, share, size, run):
    width = max(share, 128)
    for block in range(size // width):

        @pl.when((quarter * share) // width == block)
        def _():
            row = lax.broadcasted_iota(jnp.int32, (share, width), 0)
            lane = lax.broadcasted_iota(jnp.int32, (share, width), 1)
            run(slice(block * width, (block + 1) * width), lane == row + quarter * share - block * width)


def central_own_kernel(share, count, half_ref, own, found_ref, keep_ref, send_ref):
    _, core, side = position()
    size = half_ref.shape[0]
    total = central_product(half_ref, own, core, share, count) + found_ref[...]
    for step in range(count // 2):
        low, high = total[2 * step], total[2 * step + 1]
        keep_ref[step] = jnp.where(side == 0, low, high)
        send = jnp.where(side == 0, high, low)
        rounded = send.astype(BF16)
        send_ref[step, :share, :] = rounded
        send_ref[step, share:, :] = jnp.zeros((send_ref.shape[1] - share, size), BF16)

        def store(cols, mask):
            rest = jnp.where(mask, send[:, cols] - rounded[:, cols].astype(F32), 0.0)
            rest = jnp.sum(rest, axis=0, keepdims=True)
            rest = jnp.broadcast_to(rest, (send_ref.shape[1] - share, rest.shape[1]))
            send_ref[step, share:, : rest.shape[1]] = rest.astype(BF16)

        diagonal_tiles((2 * step + 1 - side) * 2 + core, share, size, store)


def direct_own_kernel(share, count, half_ref, found_ref, earlier_ref, ahead_ref, keep_ref, send_ref):
    _, core, side = position()
    for k in range(REACH):
        total = direct_product(half_ref, ahead_ref.at[k], core, share, count) + found_ref[k]
        deposit(total, side, keep_ref.at[k], send_ref.at[k])


def central_sum(share, step, central_ref, found_ref, out_ref):
    _, core, side = position()
    size = central_ref.shape[-1]
    out_ref[step, :, :size] = central_ref[step] + found_ref[step, :share, :].astype(F32)

    def add(cols, mask):
        width = mask.shape[1]
        rest = found_ref[step, share : share + 16, :width].astype(F32)[0:1]
        out_ref[step, :, cols] += jnp.where(mask, jnp.broadcast_to(rest, mask.shape), 0.0)

    diagonal_tiles((2 * step + side) * 2 + core, share, size, add)


def joined_kernel(share, central_ref, found_ref, keep_ref, direct_ref, out_ref):
    size = keep_ref.shape[-1]
    for step in range(found_ref.shape[0]):
        central_sum(share, step, central_ref, found_ref, out_ref)
        for k in range(REACH):
            cols = slice((k + 1) * size, (k + 2) * size)
            out_ref[step, :, cols] = keep_ref[k, step] + direct_ref[k, step].astype(F32)


def ready_kernel(share, central_ref, found_ref, keep_ref, one, two, out_hbm, rest_ref, block_ref, sem):
    size = keep_ref.shape[-1]
    central_sum(share, 0, central_ref, found_ref, block_ref)
    copy = pltpu.make_async_copy(block_ref, out_hbm.at[:, :, :size], sem)
    copy.start()
    for k, block in enumerate((one, two)):
        rest_ref[k] = keep_ref[k, 0] + block[...].astype(F32)
    copy.wait()


def final_kernel(earlier_hbm, rest_ref, direct_ref, out_hbm, block_ref, sems):
    size = rest_ref.shape[-1]
    copies = []
    for k in range(REACH):
        block_ref[k] = (rest_ref[k] + direct_ref[k, 0].astype(F32))[None]
        cols = slice((k + 1) * size, (k + 2) * size)
        copy = pltpu.make_async_copy(block_ref.at[k], out_hbm.at[:, :, cols], sems.at[k])
        copy.start()
        copies.append(copy)
    for copy in copies:
        copy.wait()


def shape(dims, kind=F32):
    return jax.ShapeDtypeStruct(dims, kind)


def body(basis_values, density, screen, atom_of_block, atom_factor, quad_weight, core_density):
    rows, cols = lax.axis_size("row"), lax.axis_size("col")
    col = lax.axis_index("col")
    components, row_count, points = basis_values.shape
    sb, gb = row_count // screen.shape[0], points // screen.shape[1]
    eighth = max(1, screen.shape[1] // 8) * gb
    widths = (points - 3 * eighth, 2 * eighth, eighth)
    chunks = len(widths)
    share, count = row_count // cols, cols // 2
    square = 2 * row_count * row_count

    own, *mine = call(
        functools.partial(mask_kernel, sb, gb),
        [shape((row_count, width), BF16) for width in (points, *widths)],
        [pl.BlockSpec(memory_space=pltpu.HBM)] * 2, row_count * points, 6 * row_count * points,
        scratch=[
            pltpu.SMEM(screen.shape, jnp.int32),
            pltpu.VMEM((row_count, points), BF16),
            pltpu.SemaphoreType.DMA,
            pltpu.SemaphoreType.DMA((screen.shape[0],)),
        ],
    )(pltpu.with_memory_space_constraint(screen, pltpu.HBM), pltpu.with_memory_space_constraint(basis_values, pltpu.HBM))
    near, far, across = [], [], []
    for chunk, block in enumerate(mine):
        near.append(from_side(block, 2))
        far.append(from_side(block, -2))
        across.append(swap(near[chunk], "row", 1))
    beside = swap(own, "row", 1)

    high, low = call(
        split_kernel, [shape((BAND, row_count, row_count), BF16)] * 2, [WHOLE],
        density.size * 4, density.size * 8,
    )(density)
    masked = call(
        functools.partial(widen_kernel, sb, gb), shape(basis_values.shape), [SCALARS, WHOLE],
        basis_values.size, 6 * basis_values.size,
    )(screen, basis_values)
    sums, first = [], 0
    for chunk, width in enumerate(widths):
        total = shape((row_count, width))
        partial = call(
            functools.partial(early_kernel, first), total, [WHOLE] * 5,
            6 * square * width, 10 * square,
        )(high, low, own, beside, near[chunk])
        partial = call(later_kernel, total, [WHOLE] * 4, 2 * square * width, 4 * square)(
            high, low, partial, across[chunk]
        )
        found = call(
            functools.partial(sums_kernel, first), shape((components, width)),
            [WHOLE] * 5, 2 * square * width, 6 * square,
            scratch=[pltpu.VMEM((row_count, width), F32)],
        )(high, low, partial, far[chunk], masked)
        sums.append(found)
        first += width
    ahead, behind = call(
        functools.partial(sorted_kernel, chunks),
        [shape((REACH, row_count, points), BF16)] * 2, [WHOLE] * (1 + 3 * chunks),
        row_count * points, 16 * row_count * points,
    )(beside, *near, *far, *across)
    summed = jnp.concatenate(sums, axis=1)
    groups = [(1, 2, 3)] + [(1 << bit,) for bit in range(2, rows.bit_length() - 1)]
    for group in groups:
        found = []
        for distance in group:
            found.append(swap(summed, "row", distance))
        for other in found:
            summed = summed + other

    point_density = summed[0]
    gradient = 2.0 * summed[1:]
    squared = jnp.sum(gradient * gradient, axis=0)
    atoms = atom_factor.shape[0]
    chooser = (atom_of_block[:, None] == jnp.arange(atoms, dtype=jnp.int32)[None, :]).astype(F32)
    block_factor = jnp.dot(chooser, atom_factor, precision=lax.Precision.HIGHEST)
    group_size = points // atom_of_block.shape[0]
    weights = (quad_weight.reshape(-1, group_size) * block_factor[:, None]).reshape(
        points
    ) / math.sqrt(points * cols)
    density_pot, gradient_pot = potentials(point_density, squared, core_density)
    scalar_part = 0.5 * weights * density_pot
    vector_part = 2.0 * weights * gradient_pot * gradient
    parts = jnp.concatenate([scalar_part[None], vector_part], axis=0)
    product = 2 * row_count * points * share * count
    kept = count // 2
    block = (count, share, row_count)
    fused = 1
    half, *mirrored_other = call(
        functools.partial(half_kernel, share, count, 256),
        [shape((row_count, points), BF16)] + [shape(block)] * fused, [WHOLE] * 3,
        8 * basis_values.size + fused * product, 4 * basis_values.size,
    )(masked, parts, behind)
    mirrored_found, earlier = {}, half
    for k in (2, 1):
        if k > REACH - fused:
            earlier = mirrored_other[REACH - k]
        else:
            earlier = call(
                functools.partial(mirrored_other_kernel, share, count, k - 1), shape(block),
                [WHOLE, ANYWHERE, WHOLE], product, 3 * half.size,
            )(half, earlier, behind)
        mirrored_found[k] = swap(earlier, "col", 1)
    central_other = call(
        functools.partial(central_other_kernel, share, count), shape(block),
        [WHOLE] * 2 + [ANYWHERE], 2 * product, 4 * half.size,
    )(half, own, earlier)
    central_found = swap(central_other, "col", 1)
    mirrored_keep, mirrored_send = {}, {}
    for k in (2, 1):
        mirrored_keep[k], mirrored_send[k] = call(
            functools.partial(mirrored_own_kernel, share, count, k - 1),
            [shape((kept, share, row_count)), shape((kept, share, row_count), BF16)],
            [WHOLE] * 3, product, 4 * half.size,
        )(half, mirrored_found[k], behind)
    direct_other = call(
        functools.partial(direct_other_kernel, share, count), shape((REACH, *block)),
        [WHOLE, ANYWHERE, WHOLE], product * 2, 4 * half.size,
    )(half, central_other, ahead)
    direct_found = swap(direct_other, "col", 1)
    central_keep, central_send = call(
        functools.partial(central_own_kernel, share, count),
        [
            shape((kept, share, row_count)),
            shape((kept, share + 16, row_count), BF16),
        ],
        [WHOLE] * 3, product * 2, 4 * half.size,
    )(half, own, central_found)
    central_found = swap(central_send, "col", 2)
    direct_keep, direct_send = call(
        functools.partial(direct_own_kernel, share, count),
        [
            shape((REACH, kept, share, row_count)),
            shape((REACH, kept, share, row_count), BF16),
        ],
        [WHOLE] * 2 + [ANYWHERE, WHOLE], product * 2, 4 * half.size,
    )(half, direct_found, central_keep, ahead)

    def scatter(total, axis):
        bit = 4
        while bit < cols:
            paired = total.reshape(*total.shape[:axis], -1, 2, *total.shape[axis + 1 :])
            mine = (col // bit) % 2
            keep = lax.dynamic_index_in_dim(paired, mine, axis + 1, keepdims=False)
            send = lax.dynamic_index_in_dim(paired, 1 - mine, axis + 1, keepdims=False)
            total = keep + swap(send, "col", bit)
            bit *= 2
        return total

    mirrored = []
    for k in (2, 1):
        found = swap(mirrored_send[k], "col", 2)
        total = scatter(mirrored_keep[k] + found.astype(F32), 0).astype(BF16)
        mirrored.insert(0, from_ahead(total[0], k))
    found = swap(direct_send, "col", 2)
    partial = (central_keep, central_found, direct_keep, found)
    if kept > 1:
        total = call(
            functools.partial(joined_kernel, share), shape((kept, share, 3 * row_count)),
            [WHOLE] * 4, direct_keep.size, 8 * direct_keep.size,
        )(*partial)
        total = scatter(total, 0)[0]
        zero = jnp.zeros((share, row_count), BF16)
        return total + jnp.concatenate([zero, *mirrored], axis=1).astype(F32)
    whole = shape((1, share, 3 * row_count))
    out, rest = call(
        functools.partial(ready_kernel, share), [whole, shape((REACH, share, row_count))],
        [WHOLE] * (3 + REACH), direct_keep.size, 8 * direct_keep.size,
        out_specs=[ANYWHERE, WHOLE],
        scratch=[pltpu.VMEM((1, share, row_count), F32), pltpu.SemaphoreType.DMA],
    )(central_keep, central_found, direct_keep, *mirrored)
    return pl.pallas_call(
        final_kernel,
        out_shape=whole,
        in_specs=[ANYWHERE, WHOLE, WHOLE],
        out_specs=ANYWHERE,
        input_output_aliases={0: 0},
        scratch_shapes=[
            pltpu.VMEM((REACH, 1, share, row_count), F32),
            pltpu.SemaphoreType.DMA((REACH,)),
        ],
        compiler_params=PARAMS,
    )(out, rest, found)[0]


def solution(mesh):
    in_specs = (
        P(None, "row", "col"),
        P("row", None),
        P("row", "col"),
        P("col"),
        P(),
        P("col"),
        P("col"),
    )
    out_specs = P(("row", "col"), None)

    return jax.shard_map(body, mesh=mesh, in_specs=in_specs, out_specs=out_specs, check_vma=False)
```
